128 devices in a mesh: row: 8 (over x, core), col: 16 (over z, y).
Axes of the slice: x: 4, y: 4, z: 4, core: 2. Of those that a mesh axis runs over, the one named last changes fastest.
Arguments:
- features: bfloat16 [32768, 256], P('row'), may hold values from -6 to 6
- join_weight: bfloat16 [256, 256], replicated, may hold values from -0.375 to 0.375
- partner: int32 [32768], replicated, may hold values from 0 to 32767, as said below
- tile_index: int32 [13312], P(('row', 'col')), may hold values from 0 to 127, as said below
- tile_values: bfloat16 [13312, 256, 256], P(('row', 'col')), may hold values from 0 to 10
- pert_slot: int32 [512], P(('row', 'col')), may hold values from 0 to 103
- pert_values: bfloat16 [512, 256, 256], P(('row', 'col')), may hold values from 0 to 0.5
- routes: int32 [13312, 2], P(('row', 'col')), may hold values from 0 to 127, as said below
Outputs:
- coarse_features: bfloat16 [16384, 256], P('row')
- coarse_quarters: bfloat16 [32768, 128, 128], P(('row', 'col'))
The draws below stay inside these ranges and needn't reach their ends.
Inputs may be any that keep to these rules, and one draw needn't show every extreme that they name: `partner`: fine nodes 16384 + k * 256 + j and k * 256 + s are partners of each other, where s runs over a permutation of the 256 slots for each coarse tile k. `tile_index`: each entry is a local tile position i * 8 + j with i below 16; the entries of one device are distinct; the four devices whose row indices agree modulo 8 // 2 and whose col indices agree modulo 16 // 2 hold the same list in the same order. `routes`: every column of a row equals column 0. Among the 104 rows of one device no device number appears more than 2 times, and in every draw some device number appears exactly 2 times among one device's rows.
All inputs are finite; a program needn't handle non-finite values.
Results may differ from the reference program's by a relative error of at most 0.0052.
Values may be sent and summed in bfloat16 or wider, within the bound.
No kernel may reach another device: no remote copies, remote signals or barrier semaphores. Data moves between devices by JAX's collectives and lax.ppermute only.
A program may use at most 192 MiB of HBM per device.

```python
import math
import jax
import jax.numpy as jnp
from jax import lax

TILE = 256
FEAT = 256
TC = 8
NZ = 104
NP = 4
CAP = 2
TR = 16
NT = 128
N = 32768
NCT = 64
NC = 16384
N_ROW = 8
N_COL = 16
DEVICES = 128


def group_lists(key):
    count = N_ROW // 2 * (N_COL // 2)
    subkeys = jax.random.split(jax.random.fold_in(key, 11), count)
    slot_lists = jax.vmap(lambda subkey: jax.random.permutation(subkey, TR * TC)[:NZ])(subkeys)
    slot_lists = slot_lists.reshape(N_ROW // 2, N_COL // 2, NZ).astype(jnp.int32)
    return jnp.tile(slot_lists, (2, 2, 1))


def draw_tile_index(key, part):
    return group_lists(key).reshape(-1).astype(jnp.int32)


def draw_tile_values(key, part):
    position_list = group_lists(key)
    low_log = math.log(0.35)
    high_log = math.log(2.8)
    floor_value = 0.1
    row_factor = jnp.exp(jax.random.uniform(jax.random.fold_in(key, 12), (N, N_COL), jnp.float32, low_log, high_log))
    col_factor = jnp.exp(jax.random.uniform(jax.random.fold_in(key, 14), (N, N_ROW), jnp.float32, low_log, high_log))
    row_ids = jnp.arange(N_ROW, dtype=jnp.int32)[:, None, None]
    col_ids = jnp.arange(N_COL, dtype=jnp.int32)[None, :, None]
    row_tiles = row_ids * TR + position_list // TC
    col_tiles = col_ids * TC + position_list % TC
    offsets = jnp.arange(TILE, dtype=jnp.int32)
    row_nodes = row_tiles[..., None] * TILE + offsets
    col_nodes = col_tiles[..., None] * TILE + offsets
    row_scale = row_factor[row_nodes, col_ids[..., None]]
    col_scale = col_factor[col_nodes, row_ids[..., None]]
    noise = jax.random.uniform(jax.random.fold_in(key, 13), (N_ROW, N_COL, NZ, TILE, TILE), jnp.float32, floor_value, 1.0)
    result = jnp.minimum(noise * row_scale[..., :, None] * col_scale[..., None, :], 10.0)
    return result.reshape(N_ROW * N_COL * NZ, TILE, TILE).astype(jnp.bfloat16)


def draw_partner(key, part):
    subkeys = jax.random.split(jax.random.fold_in(key, 21), NCT)
    slot_perms = jax.vmap(lambda subkey: jax.random.permutation(subkey, TILE))(subkeys).astype(jnp.int32)
    inverse = jnp.argsort(slot_perms, axis=1).astype(jnp.int32)
    tile_start = (jnp.arange(NCT, dtype=jnp.int32) * TILE)[:, None]
    first_half = NC + tile_start + inverse
    second_half = tile_start + slot_perms
    return jnp.concatenate([first_half.reshape(-1), second_half.reshape(-1)]).astype(jnp.int32)


def device_routes(subkey):
    devices = N_ROW * N_COL
    base_key = jax.random.fold_in(subkey, 1)
    busy = jax.random.randint(jax.random.fold_in(subkey, 2), (), 0, devices).astype(jnp.int32)
    weights = jax.random.randint(base_key, (devices,), 1, 64).astype(jnp.int32)
    weights = weights * weights
    slot_pool = jnp.repeat(jnp.arange(devices, dtype=jnp.int32), CAP, total_repeat_length=devices * CAP)
    pool_weight = jnp.repeat(weights, CAP, total_repeat_length=devices * CAP)
    within = jnp.tile(jnp.arange(CAP, dtype=jnp.int32), devices)
    noise = jax.random.randint(jax.random.fold_in(subkey, 3), (devices * CAP,), 0, 4096).astype(jnp.int32)
    score = pool_weight * 4096 + noise
    score = jnp.where(slot_pool == busy, 2 ** 30 - within, score)
    score = score * (devices * CAP) + jnp.arange(devices * CAP, dtype=jnp.int32)
    order = jnp.argsort(-score, stable=True)[:NZ]
    picked = slot_pool[order]
    shuffle = jax.random.permutation(jax.random.fold_in(subkey, 4), NZ)
    return picked[shuffle].astype(jnp.int32)


def draw_routes(key, part):
    devices = N_ROW * N_COL
    subkeys = jax.random.split(jax.random.fold_in(key, 31), devices)
    targets = jax.vmap(device_routes)(subkeys).reshape(-1)
    return jnp.broadcast_to(targets[:, None], (devices * NZ, CAP)).astype(jnp.int32)


def plant(values, rng, smallest, top_value):
    extent = values.shape
    spot = [jax.random.randint(jax.random.fold_in(rng, axis), (), 0, extent[axis]) for axis in range(len(extent))]
    values = values.at[tuple(spot)].set(smallest)
    longest = extent.index(max(extent))
    spot[longest] = (spot[longest] + 1) % extent[longest]
    return values.at[tuple(spot)].set(top_value)


def levels(key, extent, cuts, smallest, top_value):
    level, own = 1.0, jax.random.fold_in(key, 6)
    for dim, parts in cuts:
        heights = jnp.exp(jax.random.uniform(jax.random.fold_in(own, dim), (parts,), jnp.float32, smallest / len(cuts), top_value / len(cuts)))
        level = level * jnp.repeat(heights, extent[dim] // parts).reshape([-1 if axis == dim else 1 for axis in range(len(extent))])
    return level


def centred(own_key, shape, spread, most, cuts=(), held_as=jnp.bfloat16):
    values = jax.random.normal(own_key, shape, jnp.float32) * spread
    if len(cuts) > 0:
        values = levels(own_key, shape, cuts, -0.22, 0.18) * values
    return jnp.clip(values, min=-most, max=most).astype(held_as)


def setup_inputs(seed: int = 0) -> dict:
    key_of = jax.random.split(jax.random.key(seed), 9)
    features = centred(key_of[0], (N, FEAT), 1.0, 6.0, ((0, 8),))
    join_weight = centred(key_of[1], (FEAT, FEAT), FEAT ** -0.5, 0.375)
    partner = draw_partner(jax.random.fold_in(key_of[8], 71), 0)
    tile_index = draw_tile_index(jax.random.fold_in(key_of[8], 71), 0)
    tile_values = draw_tile_values(jax.random.fold_in(key_of[8], 71), 0)
    pert_slot = plant(jax.random.randint(key_of[5], (DEVICES * NP,), 0, NZ), jax.random.fold_in(key_of[5], 1), 0, NZ - 1).astype(jnp.int32)
    pert_values = jnp.clip(0.5 * jax.random.uniform(key_of[6], (DEVICES * NP, TILE, TILE), jnp.float32) ** levels(key_of[6], (DEVICES * NP, TILE, TILE), ((0, 128),), -0.2, 0.2), 0.0, 0.5).astype(jnp.bfloat16)
    routes = draw_routes(jax.random.fold_in(key_of[8], 71), 0)
    return dict(features=features, join_weight=join_weight, partner=partner, tile_index=tile_index, tile_values=tile_values, pert_slot=pert_slot, pert_values=pert_values, routes=routes)


def group_pairing(partner):
    odd_slots = partner[NC:].reshape(NCT, TILE) - (jnp.arange(NCT, dtype=jnp.int32) * TILE)[:, None]
    return jnp.argsort(odd_slots, axis=1).astype(jnp.int32)

def reference(features, join_weight, partner, tile_index, tile_values, pert_slot, pert_values, routes):
    half_tile = TILE // 2
    row_half = N_ROW // 2
    col_half = N_COL // 2
    groups = row_half * col_half
    inverse = group_pairing(partner)
    values = tile_values.reshape(N_ROW, N_COL, NZ, TILE, TILE)
    indices = tile_index.reshape(N_ROW, N_COL, NZ)
    extra_values = pert_values.reshape(N_ROW, N_COL, NP, TILE, TILE)
    extra_slots = pert_slot.reshape(N_ROW, N_COL, NP)

    def group_total(group_id):
        group_row = group_id // col_half
        group_col = group_id % col_half
        coarse_total = jnp.zeros((NZ, TILE, TILE), jnp.float32)
        for side_row in range(2):
            for side_col in range(2):
                row_pos = side_row * row_half + group_row
                col_pos = side_col * col_half + group_col
                tile_block = values[row_pos, col_pos].astype(jnp.float32)
                tile_block = tile_block.at[extra_slots[row_pos, col_pos]].add(extra_values[row_pos, col_pos].astype(jnp.float32))
                tile_block = tile_block.astype(jnp.bfloat16)
                local_tiles = indices[row_pos, col_pos]
                coarse_row = group_row * TR + local_tiles // TC
                coarse_col = group_col * TC + local_tiles % TC
                if side_row == 1:
                    row_pick = jnp.broadcast_to(inverse[coarse_row][:, :, None], tile_block.shape)
                    tile_block = jnp.take_along_axis(tile_block, row_pick, axis=1)
                if side_col == 1:
                    col_pick = jnp.broadcast_to(inverse[coarse_col][:, None, :], tile_block.shape)
                    tile_block = jnp.take_along_axis(tile_block, col_pick, axis=2)
                coarse_total = coarse_total + tile_block.astype(jnp.float32)
        local_tiles = indices[group_row, group_col]
        return (coarse_total, group_row * TR + local_tiles // TC, group_col * TC + local_tiles % TC)

    def group_sums(group_id):
        coarse_total, coarse_row, coarse_col = group_total(group_id)
        return (lax.optimization_barrier(jnp.sum(coarse_total, axis=2)), coarse_row)
    group_ids = jnp.arange(groups, dtype=jnp.int32)
    row_sums, row_tiles = lax.map(group_sums, group_ids)
    summed = jnp.zeros((NCT, TILE), jnp.float32).at[row_tiles.reshape(-1)].add(row_sums.reshape(-1, TILE))
    degree = 1.0 + summed / NC

    def group_quarters(group_id):
        coarse_total, coarse_row, coarse_col = group_total(group_id)
        pieces = []
        for side_row in range(2):
            for side_col in range(2):
                row_deg = degree[coarse_row][:, side_row * half_tile:(side_row + 1) * half_tile]
                col_deg = degree[coarse_col][:, side_col * half_tile:(side_col + 1) * half_tile]
                quarter = coarse_total[:, side_row * half_tile:(side_row + 1) * half_tile, side_col * half_tile:(side_col + 1) * half_tile]
                pieces.append((quarter / jnp.sqrt(row_deg[:, :, None] * col_deg[:, None, :])).astype(jnp.bfloat16))
        return jnp.stack(pieces).reshape(2, 2, NZ, half_tile, half_tile)
    quarters = lax.map(group_quarters, group_ids)
    targets = routes[:, 0].reshape(N_ROW * N_COL, NZ)
    slot_order = jnp.arange(NZ, dtype=jnp.int32)
    earlier = lax.optimization_barrier(jnp.sum(((targets[:, :, None] == targets[:, None, :]) & (slot_order[None, None, :] < slot_order[None, :, None])).astype(jnp.int32), axis=2))
    sender = (jnp.arange(2, dtype=jnp.int32)[None, :, None] * row_half + (group_ids // col_half)[:, None, None]) * N_COL
    sender = sender + jnp.arange(2, dtype=jnp.int32)[None, None, :] * col_half + (group_ids % col_half)[:, None, None]
    sender = jnp.broadcast_to(sender[..., None], (groups, 2, 2, NZ)).astype(jnp.int32)
    slot_ids = jnp.broadcast_to(slot_order, (groups, 2, 2, NZ))
    receiver = targets[sender, slot_ids]
    position = sender * CAP + earlier[sender, slot_ids]
    delivered = jnp.zeros((N_ROW * N_COL, N_ROW * N_COL * CAP, half_tile, half_tile), jnp.bfloat16)
    delivered = delivered.at[receiver, position].set(quarters)
    coarse_quarters = delivered.reshape(-1, half_tile, half_tile)
    node_tiles = features.reshape(NT, TILE, FEAT)
    feat_pick = jnp.broadcast_to(inverse[:, :, None], (NCT, TILE, FEAT))
    second_half = jnp.take_along_axis(node_tiles[NCT:], feat_pick, axis=1)
    merged = (node_tiles[:NCT].astype(jnp.float32) + second_half.astype(jnp.float32)).astype(jnp.bfloat16)
    joined_rows = jnp.dot(merged.reshape(NC, FEAT), join_weight, preferred_element_type=jnp.float32).reshape(NCT, TILE, FEAT)
    scaled = (joined_rows / jnp.sqrt(degree)[:, :, None]).astype(jnp.bfloat16)
    coarse_features = scaled.reshape(NCT, 2, half_tile, FEAT).transpose(1, 0, 2, 3).reshape(NC, FEAT)
    return (coarse_features, coarse_quarters)
```

```python
import functools

import jax
import jax.numpy as jnp
from jax import lax
from jax.experimental import pallas as pl
from jax.experimental.pallas import tpu as pltpu
from jax.sharding import PartitionSpec as P

TILE = 256
HALF = 128
STEP = 4
ROW_FIRST = 48
CHUNKS = (12, 36), (12, 44)
BF16 = jnp.bfloat16
F32 = jnp.float32


def flipped(value, axis, mask):
    pairs = [(source, source ^ mask) for source in range(lax.axis_size(axis))]
    return lax.ppermute(value, axis, pairs)


def full(shape):
    return pl.BlockSpec(shape, lambda *_: (0,) * len(shape))


def iota(shape, axis):
    return lax.broadcasted_iota(jnp.int32, shape, axis)


def sizes():
    row_half = lax.axis_size("row") // 2
    col_half = lax.axis_size("col") // 2
    return row_half, col_half


def position():
    row_half, col_half = sizes()
    row_index = lax.axis_index("row")
    col_index = lax.axis_index("col")
    return (
        lax.div(row_index, row_half),
        lax.rem(row_index, row_half),
        lax.div(col_index, col_half),
        lax.rem(col_index, col_half),
    )


def table_kernel(partner_ref, row_tables, col_tables):
    row_side, row_group, col_side, col_group = position()
    tiles_row = row_tables.shape[0]
    tiles_col = col_tables.shape[0]
    coarse_nodes = partner_ref.shape[0] * HALF // 2
    rotated = (iota((1, TILE), 1) + HALF) & (TILE - 1)
    level = iota((TILE, TILE), 0)

    def vector(start, shift):
        first = partner_ref[pl.ds(start, 1), :]
        second = partner_ref[pl.ds(start + 1, 1), :]
        return jnp.concatenate([first, second], axis=1) - shift

    def table(values):
        return (jnp.broadcast_to(values, (TILE, TILE)) == level).astype(F32).astype(BF16)

    for i in range(tiles_row):
        k = row_group * tiles_row + i
        slots = vector(coarse_nodes // HALF + 2 * k, k * TILE)
        row_tables[i] = table(jnp.where(row_side == 1, slots, rotated))
    for j in range(tiles_col):
        k = col_group * tiles_col + j
        nodes = vector(2 * k, coarse_nodes + k * TILE)
        col_tables[j] = table(jnp.where(col_side == 1, nodes, rotated))


def make_tables(partner, tiles_row, tiles_col):
    return pl.pallas_call(
        table_kernel,
        out_shape=(
            jax.ShapeDtypeStruct((tiles_row, TILE, TILE), BF16),
            jax.ShapeDtypeStruct((tiles_col, TILE, TILE), BF16),
        ),
        name="tables",
    )(partner.reshape(-1, HALF))


def pair_kernel(
    row_first, start, tiles_col,
    index_ref, pert_ref, tiles, perts, row_tables, col_tables,
    given, kept, sums, work,
):
    step = pl.program_id(0)
    count = pert_ref.shape[0]

    @pl.when(step == 0)
    def _():
        sums[...] = jnp.zeros_like(sums)

    for t in range(STEP):
        n = start + step * STEP + t
        work[t] = tiles[t]
        hits = sum((pert_ref[p] == n).astype(jnp.int32) for p in range(count))

        @pl.when(hits > 0)
        def _():
            total = tiles[t].astype(F32)
            for p in range(count):
                total = total + jnp.where(pert_ref[p] == n, perts[p].astype(F32), 0.0)
            work[t] = total.astype(BF16)

    ones = jnp.ones((8, TILE), BF16)
    for t in range(STEP):
        n = start + step * STEP + t
        place = index_ref[n]
        i = lax.div(place, tiles_col)
        j = lax.rem(place, tiles_col)
        rows = jnp.dot(row_tables[i], work[t], preferred_element_type=F32).astype(BF16)
        added = lax.dot_general(ones, rows, (((1,), (1,)), ((), ())), preferred_element_type=F32)
        sums[i] = sums[i] + added
        both = jnp.dot(rows, col_tables[j], preferred_element_type=F32).astype(BF16)
        if row_first:
            given[t] = both[:HALF]
            kept[t] = both[HALF:]
        else:
            given[t] = both[:, :HALF]
            kept[t] = both[:, HALF:]


def pair_tiles(row_first, start, count, tile_index, pert_slot, tile_values, pert_values, tables):
    row_tables, col_tables = tables
    tiles_row = row_tables.shape[0]
    tiles_col = col_tables.shape[0]
    shape = (HALF, TILE) if row_first else (TILE, HALF)
    block = pl.BlockSpec((STEP,) + shape, lambda s, *_: (s, 0, 0))
    half = jax.ShapeDtypeStruct((count,) + shape, BF16)
    return pl.pallas_call(
        functools.partial(pair_kernel, row_first, start, tiles_col),
        out_shape=(half, half, jax.ShapeDtypeStruct((tiles_row, 8, TILE), F32)),
        grid_spec=pltpu.PrefetchScalarGridSpec(
            num_scalar_prefetch=2,
            grid=(count // STEP,),
            in_specs=[
                pl.BlockSpec((STEP, TILE, TILE), lambda s, *_: (s + start // STEP, 0, 0)),
                full(pert_values.shape),
                full(row_tables.shape),
                full(col_tables.shape),
            ],
            out_specs=(block, block, full((tiles_row, 8, TILE))),
            scratch_shapes=[pltpu.VMEM((STEP, TILE, TILE), BF16)],
        ),
        name="pair_rows" if row_first else "pair_cols",
    )(tile_index, pert_slot, tile_values, pert_values, row_tables, col_tables)


def forward_kernel(kept, came, given):
    given[...] = (kept[...].astype(F32) + came[...].astype(F32)).astype(BF16)


def forward(kept, came):
    count = kept.shape[0]
    part = max(d for d in range(1, 13) if count % d == 0)
    block = pl.BlockSpec((part, HALF, HALF), lambda s: (s, 0, 0))
    return pl.pallas_call(
        forward_kernel,
        out_shape=jax.ShapeDtypeStruct((count, HALF, HALF), BF16),
        grid=(count // part,),
        in_specs=[block, block],
        out_specs=block,
        name="forward",
    )(kept, came)


def zero_kernel(_, out):
    out[...] = jnp.zeros_like(out)


def zero_buffer(anchor, count):
    return pl.pallas_call(
        zero_kernel,
        out_shape=jax.ShapeDtypeStruct((count, HALF, HALF), BF16),
        grid=(count // 32,),
        in_specs=[pl.BlockSpec(memory_space=pl.ANY)],
        out_specs=pl.BlockSpec((32, HALF, HALF), lambda s: (s, 0, 0)),
        name="zero_buffer",
    )(anchor)


def inverse_root(raw):
    half = raw.shape[0] // 2
    total = raw[:half] + raw[half:]
    degree = 1.0 + total / (total.shape[0] * total.shape[1])
    return 1.0 / jnp.sqrt(degree)


def picked(scale, k, side):
    return scale[side, pl.ds(k, 1), :]


def upright(line):
    return jnp.broadcast_to(line, (HALF, HALF)).T


def finish_kernel(
    start, tiles_row, tiles_col,
    index_ref, place_ref, kept, came, last, raw, _, out, scale, row_scale, col_scale, done, sem,
):
    step = pl.program_id(0)
    steps = pl.num_programs(0)

    @pl.when(step == 0)
    def _():
        row_side, row_group, col_side, col_group = position()
        roots = inverse_root(raw[...])
        scale[0] = roots[:, :HALF]
        scale[1] = roots[:, HALF:]
        for i in range(tiles_row):
            row_scale[i] = upright(picked(scale, row_group * tiles_row + i, row_side))
        for j in range(tiles_col):
            col_scale[j] = jnp.broadcast_to(
                picked(scale, col_group * tiles_col + j, col_side), (8, HALF)
            )

    for t in range(STEP):
        m = step * STEP + t
        place = index_ref[start + m]
        i = lax.div(place, tiles_col)
        j = lax.rem(place, tiles_col)
        total = kept[t].astype(F32) + came[t].astype(F32) + last[t].astype(F32)
        done[m] = (total * row_scale[i] * col_scale[j, 0:1]).astype(BF16)
        pltpu.make_async_copy(done.at[m], out.at[place_ref[start + m]], sem).start()

    @pl.when(step == steps - 1)
    def _():
        pltpu.make_async_copy(done, out.at[pl.ds(0, done.shape[0])], sem).wait()


def finish(row_first, start, tile_index, place, kept, came, last, raw, buffer, tiles_row, tiles_col):
    count = kept.shape[0]
    if row_first:
        second = pl.BlockSpec((STEP, HALF, HALF), lambda s, *_: (s, 0, 1))
    else:
        second = pl.BlockSpec((STEP, HALF, HALF), lambda s, *_: (s, 1, 0))
    anywhere = pl.BlockSpec(memory_space=pl.ANY)
    return pl.pallas_call(
        functools.partial(finish_kernel, start, tiles_row, tiles_col),
        out_shape=jax.ShapeDtypeStruct(buffer.shape, BF16),
        grid_spec=pltpu.PrefetchScalarGridSpec(
            num_scalar_prefetch=2,
            grid=(count // STEP,),
            in_specs=[
                second,
                second,
                pl.BlockSpec((STEP, HALF, HALF), lambda s, *_: (s, 0, 0)),
                full(raw.shape),
                anywhere,
            ],
            out_specs=anywhere,
            scratch_shapes=[
                pltpu.VMEM((2, raw.shape[0] // 2, HALF), F32),
                pltpu.VMEM((tiles_row, HALF, HALF), F32),
                pltpu.VMEM((tiles_col, 8, HALF), F32),
                pltpu.VMEM((count, HALF, HALF), BF16),
                pltpu.SemaphoreType.DMA,
            ],
        ),
        input_output_aliases={6: 0},
        name="finish_rows" if row_first else "finish_cols",
    )(tile_index, place, kept, came, last, raw, buffer)


def feature_kernel(lane_ref, tiles, tables, given, kept):
    for t in range(tiles.shape[0]):
        rows = jnp.dot(tables[t], tiles[t], preferred_element_type=F32).astype(BF16)
        given[t] = rows[:HALF]
        kept[t] = rows[HALF:]


def pair_features(lane, tiles, row_tables, part):
    width = tiles.shape[2]
    half = jax.ShapeDtypeStruct((part, HALF, width), BF16)
    return pl.pallas_call(
        feature_kernel,
        out_shape=(half, half),
        grid_spec=pltpu.PrefetchScalarGridSpec(
            num_scalar_prefetch=1,
            grid=(1,),
            in_specs=[
                pl.BlockSpec((part, TILE, width), lambda s, lane: (lane[0], 0, 0)),
                pl.BlockSpec((part, TILE, TILE), lambda s, lane: (lane[0], 0, 0)),
            ],
            out_specs=(full((part, HALF, width)), full((part, HALF, width))),
        ),
        name="pair_features",
    )(lane, tiles, row_tables)


def join_kernel(tiles_row, lane_ref, kept, came, weight, raw, out, scale):
    row_side, row_group, _, _ = position()
    part = kept.shape[0]
    roots = inverse_root(raw[...])
    scale[0] = roots[:, :HALF]
    scale[1] = roots[:, HALF:]
    for t in range(part):
        merged = (kept[t].astype(F32) + came[t].astype(F32)).astype(BF16)
        joined = jnp.dot(merged, weight[...], preferred_element_type=F32)
        k = row_group * tiles_row + lane_ref[0] * part + t
        column = upright(picked(scale, k, row_side))
        width = joined.shape[1] // HALF
        out[t] = (joined * jnp.concatenate([column] * width, axis=1)).astype(BF16)


def join_features(lane, kept, came, weight, raw, tiles_row):
    return pl.pallas_call(
        functools.partial(join_kernel, tiles_row),
        out_shape=jax.ShapeDtypeStruct(kept.shape, BF16),
        grid_spec=pltpu.PrefetchScalarGridSpec(
            num_scalar_prefetch=1,
            grid=(1,),
            in_specs=[full(kept.shape), full(kept.shape), full(weight.shape), full(raw.shape)],
            out_specs=full(kept.shape),
            scratch_shapes=[pltpu.VMEM((2, raw.shape[0] // 2, HALF), F32)],
        ),
        name="join_features",
    )(lane, kept, came, weight, raw)


def local(features, join_weight, partner, tile_index, tile_values, pert_slot, pert_values, routes):
    row_count = lax.axis_size("row")
    col_count = lax.axis_size("col")
    devices = row_count * col_count
    row_mask = row_count // 2
    col_mask = col_count // 2
    slot_count = tile_values.shape[0]
    width = features.shape[1]
    tiles_row = features.shape[0] // TILE
    tiles_col = partner.shape[0] // TILE // col_count
    capacity = routes.shape[1]
    lanes = 4
    part = tiles_row // lanes
    row_side = lax.axis_index("row") // row_mask
    lane = (lax.axis_index("col") % lanes).reshape(1)

    tables = make_tables(partner, tiles_row, tiles_col)

    pieces = []
    starts = [0, ROW_FIRST]
    for chunk in range(len(CHUNKS[0])):
        for kind in range(2):
            row_first = kind == 0
            count = CHUNKS[kind][chunk]
            given, kept, sums = pair_tiles(
                row_first, starts[kind], count, tile_index, pert_slot, tile_values, pert_values, tables
            )
            came = flipped(given, "row", row_mask) if row_first else flipped(given, "col", col_mask)
            pieces.append([row_first, starts[kind], kept, came, sums])
            starts[kind] += count

    feature_given, feature_kept = pair_features(
        lane, features.reshape(tiles_row, TILE, width), tables[0], part
    )
    feature_came = flipped(feature_given, "row", row_mask)

    own = sum(piece[4][:, 0, :] for piece in pieces)
    own = jnp.where(row_side == 1, own, jnp.roll(own, HALF, axis=1))
    spread = lax.all_to_all(own, "col", split_axis=0, concat_axis=0, tiled=True)
    line = jnp.sum(spread, axis=0)
    raw = lax.all_to_all(
        jnp.broadcast_to(line[None], (devices, TILE)),
        ("row", "col"),
        split_axis=0,
        concat_axis=0,
        tiled=True,
    )

    targets = routes[:, 0]
    order = jnp.arange(slot_count, dtype=jnp.int32)
    same = (targets[:, None] == targets[None, :]) & (order[None, :] < order[:, None])
    place = targets * capacity + jnp.sum(same.astype(jnp.int32), axis=1)

    for piece in pieces:
        row_first, start, kept, came, _ = piece
        given = forward(kept, came)
        last = flipped(given, "col", col_mask) if row_first else flipped(given, "row", row_mask)
        piece.append(last)

    joined = join_features(lane, feature_kept, feature_came, join_weight, raw, tiles_row)
    parts = jnp.zeros((lanes, part, HALF, width), BF16)
    for shift in range(lanes):
        shared = joined
        if shift > 0:
            pairs = [
                (source, source // lanes * lanes + (source + shift) % lanes)
                for source in range(col_count)
            ]
            shared = lax.ppermute(joined, "col", pairs)
        parts = lax.dynamic_update_slice(
            parts, shared[None], ((lane[0] - shift) % lanes, 0, 0, 0)
        )
    coarse_features = parts.reshape(tiles_row * HALF, width)

    buffer = zero_buffer(pieces[-1][3], devices * capacity)
    for row_first, start, kept, came, _, last in pieces:
        buffer = finish(
            row_first, start, tile_index, place, kept, came, last, raw, buffer, tiles_row, tiles_col
        )
    arrived = lax.all_to_all(buffer, ("row", "col"), split_axis=0, concat_axis=0, tiled=True)
    return (coarse_features, arrived)


def solution(mesh):
    both = P(("row", "col"))
    placed = (
        P("row", None),
        P(),
        P(),
        both,
        P(("row", "col"), None, None),
        both,
        P(("row", "col"), None, None),
        P(("row", "col"), None),
    )
    return jax.shard_map(
        local,
        mesh=mesh,
        in_specs=placed,
        out_specs=(P("row", None), P(("row", "col"), None, None)),
        check_vma=False,
    )
```

```python
import functools

import jax
import jax.numpy as jnp
from jax import lax
from jax.experimental import pallas as pl
from jax.experimental.pallas import tpu as pltpu
from jax.sharding import PartitionSpec as P


TILE = 256
HALF = 128
STEP = 8
LANES = 4
ROW_FIRST = 48
CHUNKS = (8, 16), (24, 24), (16, 16)
BF16 = jnp.bfloat16
F32 = jnp.float32
PARAMS = pltpu.CompilerParams(vmem_limit_bytes=60 << 20)
ANYWHERE = pl.BlockSpec(memory_space=pl.ANY)


def flipped(value, axis, mask):
    pairs = [(source, source ^ mask) for source in range(lax.axis_size(axis))]
    return lax.ppermute(value, axis, pairs)


def full(shape):
    return pl.BlockSpec(shape, lambda *_: (0,) * len(shape))


def iota(shape, axis):
    return lax.broadcasted_iota(jnp.int32, shape, axis)


def position():
    row_half = lax.axis_size("row") // 2
    col_half = lax.axis_size("col") // 2
    row_index = lax.axis_index("row")
    col_index = lax.axis_index("col")
    return (
        lax.div(row_index, row_half),
        lax.rem(row_index, row_half),
        lax.div(col_index, col_half),
        lax.rem(col_index, col_half),
    )


def build_tables(partner_ref, row_tables, col_tables):
    row_side, row_group, col_side, col_group = position()
    tiles_row = row_tables.shape[0]
    tiles_col = col_tables.shape[0]
    coarse_nodes = partner_ref.shape[0] * HALF // 2
    rotated = (iota((1, TILE), 1) + HALF) & (TILE - 1)
    level = iota((TILE, TILE), 0)

    def vector(start, shift):
        first = partner_ref[pl.ds(start, 1), :]
        second = partner_ref[pl.ds(start + 1, 1), :]
        return jnp.concatenate([first, second], axis=1) - shift

    def table(values):
        return (jnp.broadcast_to(values, (TILE, TILE)) == level).astype(F32).astype(BF16)

    for i in range(tiles_row):
        k = row_group * tiles_row + i
        slots = vector(coarse_nodes // HALF + 2 * k, k * TILE)
        row_tables[i] = table(jnp.where(row_side == 1, slots, rotated))
    for j in range(tiles_col):
        k = col_group * tiles_col + j
        nodes = vector(2 * k, coarse_nodes + k * TILE)
        col_tables[j] = table(jnp.where(col_side == 1, nodes, rotated))


def pair_kernel(
    starts, counts, with_features, index_ref, pert_ref, lane_ref, tiles, partner_ref, perts, *rest
):
    if with_features:
        features, rest = rest[0], rest[1:]
    _, row_given, row_kept, col_given, col_kept, row_tables, col_tables, rows = rest
    tiles_col = col_tables.shape[0]
    step = pl.program_id(0)
    row_steps = counts[0] // STEP
    pert_count = pert_ref.shape[0]
    first = jnp.where(
        step < row_steps, starts[0] + step * STEP, starts[1] + (step - row_steps) * STEP
    )

    @pl.when(step == 0)
    def _():
        build_tables(partner_ref, row_tables, col_tables)

    hits = sum(
        ((pert_ref[p] >= first) & (pert_ref[p] < first + STEP)).astype(jnp.int32)
        for p in range(pert_count)
    )

    @pl.when(hits > 0)
    def _():
        for t in range(STEP):
            found = sum((pert_ref[p] == first + t).astype(jnp.int32) for p in range(pert_count))

            @pl.when(found > 0)
            def _():
                total = tiles[t].astype(F32)
                for p in range(pert_count):
                    total = total + jnp.where(pert_ref[p] == first + t, perts[p].astype(F32), 0.0)
                tiles[t] = total.astype(BF16)

    def put(t, both, given, kept, row_first):
        cross = both[:HALF, HALF:], both[HALF:, :HALF]
        given[0, t] = both[:HALF, :HALF]
        given[1, t] = cross[0 if row_first else 1]
        kept[0, t] = cross[1 if row_first else 0]
        kept[1, t] = both[HALF:, HALF:]

    def compute(given, kept, row_first):
        for t in range(STEP):
            i = lax.div(index_ref[first + t], tiles_col)
            rows[t] = jnp.dot(row_tables[i], tiles[t], preferred_element_type=F32).astype(BF16)
        for t in range(STEP):
            j = lax.rem(index_ref[first + t], tiles_col)
            both = jnp.dot(rows[t], col_tables[j], preferred_element_type=F32).astype(BF16)
            put(t, both, given, kept, row_first)

    @pl.when(step < row_steps)
    def _():
        compute(row_given, row_kept, True)
        if with_features:
            for t in range(features.shape[0]):
                table = row_tables[lane_ref[0] * features.shape[0] + t]
                both = jnp.dot(table, features[t], preferred_element_type=F32).astype(BF16)
                put(STEP + t, both, row_given, row_kept, True)

    @pl.when(step >= row_steps)
    def _():
        compute(col_given, col_kept, False)


def pair_tiles(
    starts, counts, index, pert_slot, lane, tile_values, partner, pert_values, features, sizes, token
):
    tiles_row, tiles_col = sizes
    row_steps, col_steps = counts[0] // STEP, counts[1] // STEP
    row_block, col_block = starts[0] // STEP, starts[1] // STEP
    with_features = features is not None
    extra = features.shape[0] // LANES if with_features else 0

    def tile_map(s, *_):
        return (jnp.where(s < row_steps, row_block + s, col_block + s - row_steps), 0, 0)

    shapes = [
        jax.ShapeDtypeStruct((2, count, HALF, HALF), BF16)
        for count in (counts[0] + extra,) * 2 + (counts[1],) * 2
    ]
    if with_features:
        row_out = full(shapes[0].shape)
    else:
        row_out = pl.BlockSpec(
            (2, STEP, HALF, HALF), lambda s, *_: (0, jnp.minimum(s, row_steps - 1), 0, 0)
        )
    col_out = pl.BlockSpec(
        (2, STEP, HALF, HALF), lambda s, *_: (0, jnp.maximum(s - row_steps, 0), 0, 0)
    )
    in_specs = [
        pl.BlockSpec((STEP, TILE, TILE), tile_map),
        full(partner.shape),
        full(pert_values.shape),
    ]
    operands = [tile_values, partner, pert_values]
    if with_features:
        in_specs.append(
            pl.BlockSpec((extra,) + features.shape[1:], lambda s, a, b, lane: (lane[0], 0, 0))
        )
        operands.append(features)
    return pl.pallas_call(
        functools.partial(pair_kernel, starts, counts, with_features),
        out_shape=shapes,
        grid_spec=pltpu.PrefetchScalarGridSpec(
            num_scalar_prefetch=3,
            grid=(row_steps + col_steps,),
            in_specs=in_specs + [ANYWHERE],
            out_specs=[row_out, row_out, col_out, col_out],
            scratch_shapes=[
                pltpu.VMEM((tiles_row, TILE, TILE), BF16),
                pltpu.VMEM((tiles_col, TILE, TILE), BF16),
                pltpu.VMEM((STEP, TILE, TILE), BF16),
            ],
        ),
        compiler_params=PARAMS,
        name="pair_tiles",
    )(index, pert_slot, lane, *operands, token)


def sum_kernel(bounds, tiles_col, index_ref, *rest):
    pieces, sums, total = rest[:-2], rest[-2], rest[-1]
    step = pl.program_id(0)

    @pl.when(step == 0)
    def _():
        total[...] = jnp.zeros_like(total)

    for number, (begin, steps, start, row_first) in enumerate(bounds):
        given, kept = pieces[2 * number], pieces[2 * number + 1]

        @pl.when((step >= begin) & (step < begin + steps))
        def _():
            for t in range(STEP):
                i = lax.div(index_ref[start + (step - begin) * STEP + t], tiles_col)
                cross = given[1, t].astype(F32), kept[0, t].astype(F32)
                given_part, kept_part = cross if row_first else cross[::-1]
                total[0, i] += given[0, t].astype(F32) + given_part
                total[1, i] += kept[1, t].astype(F32) + kept_part

    @pl.when(step == pl.num_programs(0) - 1)
    def _():
        row_side = position()[0]
        for i in range(total.shape[1]):
            given_line = jnp.sum(total[0, i].T, axis=0, keepdims=True)
            kept_line = jnp.sum(total[1, i].T, axis=0, keepdims=True)
            sums[i : i + 1, :HALF] = jnp.where(row_side == 1, given_line, kept_line)
            sums[i : i + 1, HALF:] = jnp.where(row_side == 1, kept_line, given_line)


def sum_rows(pieces, index, sizes):
    tiles_row, tiles_col = sizes
    bounds, specs, operands = [], [], []
    begin = 0
    for piece in pieces:
        steps = piece["count"] // STEP

        def block_map(s, *_, begin=begin, steps=steps):
            return (0, jnp.clip(s - begin, 0, steps - 1), 0, 0)

        specs += [pl.BlockSpec((2, STEP, HALF, HALF), block_map)] * 2
        operands += [piece["given"], piece["kept"]]
        bounds.append((begin, steps, piece["start"], piece["row_first"]))
        begin += steps
    return pl.pallas_call(
        functools.partial(sum_kernel, bounds, tiles_col),
        out_shape=jax.ShapeDtypeStruct((tiles_row, TILE), F32),
        grid_spec=pltpu.PrefetchScalarGridSpec(
            num_scalar_prefetch=1,
            grid=(begin,),
            in_specs=specs,
            out_specs=full((tiles_row, TILE)),
            scratch_shapes=[pltpu.VMEM((2, tiles_row, HALF, HALF), F32)],
        ),
        compiler_params=PARAMS,
        name="sum_rows",
    )(index, *operands)


def line_kernel(spread, _, out):
    line = jnp.sum(spread[...], axis=0, keepdims=True)
    out[...] = jnp.broadcast_to(line, out.shape)


def line_copies(spread, devices, token):
    return pl.pallas_call(
        line_kernel,
        out_shape=jax.ShapeDtypeStruct((devices, TILE), F32),
        in_specs=[pl.BlockSpec(memory_space=pltpu.VMEM), ANYWHERE],
        out_specs=pl.BlockSpec(memory_space=pltpu.VMEM),
        compiler_params=PARAMS,
        name="line_copies",
    )(spread, token)


def forward_kernel(steps, *refs):
    row_kept, row_came, col_kept, col_came = refs[:4]
    row_given, col_given = refs[-2:]
    step = pl.program_id(0)

    def both(kept, came, given):
        given[...] = (kept[0].astype(F32) + came[0].astype(F32)).astype(BF16)

    pl.when(step < steps[0])(lambda: both(row_kept, row_came, row_given))
    pl.when(step < steps[1])(lambda: both(col_kept, col_came, col_given))


def quadrant(which, steps):
    return pl.BlockSpec(
        (1, STEP, HALF, HALF), lambda s, *_: (which, jnp.minimum(s, steps - 1), 0, 0)
    )


def plain(steps):
    return pl.BlockSpec((STEP, HALF, HALF), lambda s, *_: (jnp.minimum(s, steps - 1), 0, 0))


def forward(pair, tokens):
    steps = [piece["count"] // STEP for piece in pair]
    operands = [piece[key] for piece in pair for key in ("kept", "came")]
    return pl.pallas_call(
        functools.partial(forward_kernel, steps),
        out_shape=[jax.ShapeDtypeStruct((piece["count"], HALF, HALF), BF16) for piece in pair],
        grid=(max(steps),),
        in_specs=[quadrant(0, steps[k // 2]) for k in range(4)] + [ANYWHERE] * len(tokens),
        out_specs=[plain(steps[0]), plain(steps[1])],
        compiler_params=PARAMS,
        name="forward",
    )(*operands, *tokens)


def zero_kernel(_, out):
    out[...] = jnp.zeros_like(out)


def zero_buffer(count, token):
    return pl.pallas_call(
        zero_kernel,
        out_shape=jax.ShapeDtypeStruct((count, HALF, HALF), BF16),
        grid=(count // 64,),
        in_specs=[ANYWHERE],
        out_specs=pl.BlockSpec((64, HALF, HALF), lambda s: (s, 0, 0)),
        compiler_params=PARAMS,
        name="zero_buffer",
    )(token)


def store_roots(raw, scale):
    half = raw.shape[0] // 2
    total = raw[:half] + raw[half:]
    roots = 1.0 / jnp.sqrt(1.0 + total / (total.shape[0] * total.shape[1]))
    scale[0] = roots[:, :HALF]
    scale[1] = roots[:, HALF:]


def upright(line):
    return jnp.broadcast_to(line, (HALF, HALF)).T


def finish_kernel(starts, counts, index_ref, place_ref, *refs):
    pieces, raw = (refs[0:3], refs[3:6]), refs[6]
    out, scale, row_scale, col_scale, done, sem = refs[-6:]
    tiles_row = row_scale.shape[0]
    tiles_col = col_scale.shape[0]
    step = pl.program_id(0)

    @pl.when(step == 0)
    def _():
        row_side, row_group, col_side, col_group = position()
        store_roots(raw, scale)
        for i in range(tiles_row):
            row_scale[i] = upright(scale[row_side, pl.ds(row_group * tiles_row + i, 1), :])
        for j in range(tiles_col):
            line = scale[col_side, pl.ds(col_group * tiles_col + j, 1), :]
            col_scale[j] = jnp.broadcast_to(line, (8, HALF))

    for number in range(2):
        kept, came, last = pieces[number]
        base = number * counts[0]

        @pl.when(step < counts[number] // STEP)
        def _():
            for t in range(STEP):
                m = step * STEP + t
                n = starts[number] + m
                i = lax.div(index_ref[n], tiles_col)
                j = lax.rem(index_ref[n], tiles_col)
                total = kept[0, t].astype(F32) + came[0, t].astype(F32) + last[t].astype(F32)
                done[base + m] = (total * row_scale[i] * col_scale[j, 0:1]).astype(BF16)
                pltpu.make_async_copy(done.at[base + m], out.at[place_ref[n]], sem).start()

    @pl.when(step == pl.num_programs(0) - 1)
    def _():
        pltpu.make_async_copy(done, out.at[pl.ds(0, done.shape[0])], sem).wait()


def finish(pair, index, place, raw, buffer, sizes, token):
    tiles_row, tiles_col = sizes
    starts = [piece["start"] for piece in pair]
    counts = [piece["count"] for piece in pair]
    specs, operands = [], []
    for piece in pair:
        steps = piece["count"] // STEP
        specs += [quadrant(1, steps), quadrant(1, steps), plain(steps)]
        operands += [piece["kept"], piece["came"], piece["last"]]
    return pl.pallas_call(
        functools.partial(finish_kernel, starts, counts),
        out_shape=jax.ShapeDtypeStruct(buffer.shape, BF16),
        grid_spec=pltpu.PrefetchScalarGridSpec(
            num_scalar_prefetch=2,
            grid=(max(counts) // STEP,),
            in_specs=specs + [full(raw.shape), ANYWHERE, ANYWHERE],
            out_specs=ANYWHERE,
            scratch_shapes=[
                pltpu.VMEM((2, raw.shape[0] // 2, HALF), F32),
                pltpu.VMEM((tiles_row, HALF, HALF), F32),
                pltpu.VMEM((tiles_col, 8, HALF), F32),
                pltpu.VMEM((sum(counts), HALF, HALF), BF16),
                pltpu.SemaphoreType.DMA,
            ],
        ),
        input_output_aliases={9: 0},
        compiler_params=PARAMS,
        name="finish",
    )(index, place, *operands, raw, buffer, token)


def join_kernel(tiles_row, lane_ref, kept, came, weight, raw, _, out, scale):
    row_side, row_group, _, _ = position()
    part = out.shape[0]
    store_roots(raw, scale)
    for t in range(part):
        merged = [
            (kept[h, t].astype(F32) + came[h, t].astype(F32)).astype(BF16) for h in range(2)
        ]
        joined = jnp.dot(
            jnp.concatenate(merged, axis=1), weight[...], preferred_element_type=F32
        )
        k = row_group * tiles_row + lane_ref[0] * part + t
        column = upright(scale[row_side, pl.ds(k, 1), :])
        out[t] = (joined * jnp.concatenate([column] * 2, axis=1)).astype(BF16)


def join_features(lane, piece, weight, raw, tiles_row, token):
    part = tiles_row // LANES
    block = pl.BlockSpec((2, part, HALF, HALF), lambda s, *_: (0, piece["count"] // part, 0, 0))
    shape = (part, HALF, weight.shape[1])
    return pl.pallas_call(
        functools.partial(join_kernel, tiles_row),
        out_shape=jax.ShapeDtypeStruct(shape, BF16),
        grid_spec=pltpu.PrefetchScalarGridSpec(
            num_scalar_prefetch=1,
            grid=(1,),
            in_specs=[block, block, full(weight.shape), full(raw.shape), ANYWHERE],
            out_specs=full(shape),
            scratch_shapes=[pltpu.VMEM((2, raw.shape[0] // 2, HALF), F32)],
        ),
        compiler_params=PARAMS,
        name="join_features",
    )(lane, piece["kept"], piece["came"], weight, raw, token)


def copy_kernel(parts, source, out, held, read_sem, write_sem):
    size = source.shape[0] // parts

    def window(k):
        return pl.ds(k * size, size)

    def read(k):
        return pltpu.make_async_copy(source.at[window(k)], held.at[window(k)], read_sem.at[k])

    def write(k):
        return pltpu.make_async_copy(held.at[window(k)], out.at[window(k)], write_sem.at[k])

    for k in range(parts):
        read(k).start()
    for k in range(parts):
        read(k).wait()
        write(k).start()
    for k in range(parts):
        write(k).wait()


def copied(source):
    parts = 16
    return pl.pallas_call(
        functools.partial(copy_kernel, parts),
        out_shape=jax.ShapeDtypeStruct(source.shape, source.dtype),
        in_specs=[ANYWHERE],
        out_specs=ANYWHERE,
        scratch_shapes=[
            pltpu.VMEM(source.shape, source.dtype),
            pltpu.SemaphoreType.DMA((parts,)),
            pltpu.SemaphoreType.DMA((parts,)),
        ],
        compiler_params=PARAMS,
        name="copied",
    )(source)


def level(features, join_weight, partner, tile_index, tile_values, pert_slot, pert_values, routes):
    row_count = lax.axis_size("row")
    col_count = lax.axis_size("col")
    devices = row_count * col_count
    masks = ("row", row_count // 2), ("col", col_count // 2)
    slot_count = tile_values.shape[0]
    width = features.shape[1]
    tiles_row = features.shape[0] // TILE
    tiles_col = partner.shape[0] // TILE // col_count
    sizes = tiles_row, tiles_col
    capacity = routes.shape[1]
    part = tiles_row // LANES
    chunks = len(CHUNKS)
    lane = (lax.axis_index("col") % LANES).reshape(1)
    partner = partner.reshape(-1, HALF)
    feature_tiles = features.reshape(tiles_row, TILE, width)

    starts = [0, ROW_FIRST]
    token = pert_values
    pairs = []
    for chunk in range(chunks):
        counts = CHUNKS[chunk]
        row_given, row_kept, col_given, col_kept = pair_tiles(
            tuple(starts), counts, tile_index, pert_slot, lane, tile_values, partner,
            pert_values, feature_tiles if chunk == 0 else None, sizes, token,
        )
        token = col_kept
        pair = []
        for kind, (given, kept) in enumerate(((row_given, row_kept), (col_given, col_kept))):
            came = flipped(given, *masks[kind])
            pair.append(
                dict(
                    row_first=kind == 0, start=starts[kind], count=counts[kind],
                    given=given, kept=kept, came=came,
                )
            )
            starts[kind] += counts[kind]
        pairs.append(pair)

    own = sum_rows([piece for pair in pairs for piece in pair], tile_index, sizes)
    token = own
    spread = lax.all_to_all(own, "col", split_axis=0, concat_axis=0, tiled=True)

    targets = routes[:, 0]
    order = jnp.arange(slot_count, dtype=jnp.int32)
    same = (targets[:, None] == targets[None, :]) & (order[None, :] < order[:, None])
    place = targets * capacity + jnp.sum(same.astype(jnp.int32), axis=1)

    for chunk, pair in enumerate(pairs):
        tokens = [token]
        if chunk == chunks - 1:
            lines = line_copies(spread, devices, token)
            raw = lax.all_to_all(
                lines, ("row", "col"), split_axis=0, concat_axis=0, tiled=True
            )
            buffer = zero_buffer(devices * capacity, lines)
            tokens = [buffer]
        given = forward(pair, tokens)
        token = given[0]
        for kind in range(2):
            pair[kind]["last"] = flipped(given[kind], *masks[1 - kind])

    def finished(chunk, buffer, token):
        return finish(pairs[chunk], tile_index, place, raw, buffer, sizes, token)

    buffer = finished(0, buffer, token)
    joined = join_features(lane, pairs[0][0], join_weight, raw, tiles_row, buffer)
    buffer = finished(1, buffer, joined)
    parts = jnp.zeros((LANES, part, HALF, width), BF16)
    for shift in range(LANES):
        shared = joined
        if shift > 0:
            ring = [
                (source, source // LANES * LANES + (source + shift) % LANES)
                for source in range(col_count)
            ]
            shared = lax.ppermute(joined, "col", ring)
        parts = lax.dynamic_update_slice(
            parts, shared[None], ((lane[0] - shift) % LANES, 0, 0, 0)
        )
    buffer = finished(2, buffer, parts)
    coarse_features = parts.reshape(tiles_row * HALF, width)
    arrived = lax.all_to_all(buffer, ("row", "col"), split_axis=0, concat_axis=0, tiled=True)
    return (coarse_features, copied(arrived))


def solution(mesh):
    both = P(("row", "col"))
    placed = (
        P("row", None),
        P(),
        P(),
        both,
        P(("row", "col"), None, None),
        both,
        P(("row", "col"), None, None),
        P(("row", "col"), None),
    )
    return jax.shard_map(
        level,
        mesh=mesh,
        in_specs=placed,
        out_specs=(P("row", None), P(("row", "col"), None, None)),
        check_vma=False,
    )
```

```python
import functools

import jax
import jax.numpy as jnp
from jax import lax
from jax.experimental import pallas as pl
from jax.experimental.pallas import tpu as pltpu
from jax.sharding import PartitionSpec as P


TILE = 256
HALF = 128
STEP = 8
LANES = 4
ROW_FIRST = 48
CHUNKS = (8, 16), (24, 24), (16, 16)
BF16 = jnp.bfloat16
F32 = jnp.float32
PARAMS = pltpu.CompilerParams(vmem_limit_bytes=66_500_000)
ANYWHERE = pl.BlockSpec(memory_space=pl.ANY)


def flipped(value, axis, mask):
    pairs = [(source, source ^ mask) for source in range(lax.axis_size(axis))]
    return lax.ppermute(value, axis, pairs)


def full(shape):
    return pl.BlockSpec(shape, lambda *_: (0,) * len(shape))


def iota(shape, axis):
    return lax.broadcasted_iota(jnp.int32, shape, axis)


def position():
    row_half = lax.axis_size("row") // 2
    col_half = lax.axis_size("col") // 2
    row_index = lax.axis_index("row")
    col_index = lax.axis_index("col")
    return (
        lax.div(row_index, row_half),
        lax.rem(row_index, row_half),
        lax.div(col_index, col_half),
        lax.rem(col_index, col_half),
    )


def build_tables(partner_ref, row_tables, col_tables):
    row_side, row_group, col_side, col_group = position()
    tiles_row = row_tables.shape[0]
    tiles_col = col_tables.shape[0]
    coarse_nodes = partner_ref.shape[0] * HALF // 2
    rotated = (iota((1, TILE), 1) + HALF) & (TILE - 1)
    level = iota((TILE, TILE), 0).astype(F32).astype(BF16)

    def vector(start, shift):
        first = partner_ref[pl.ds(start, 1), :]
        second = partner_ref[pl.ds(start + 1, 1), :]
        return jnp.concatenate([first, second], axis=1) - shift

    def table(values):
        line = values.astype(F32).astype(BF16)
        same = jnp.broadcast_to(line, (TILE, TILE)) == level
        return jnp.where(same, jnp.ones((), BF16), jnp.zeros((), BF16))

    for i in range(tiles_row):
        k = row_group * tiles_row + i
        slots = vector(coarse_nodes // HALF + 2 * k, k * TILE)
        row_tables[i] = table(jnp.where(row_side == 1, slots, rotated))
    for j in range(tiles_col):
        k = col_group * tiles_col + j
        nodes = vector(2 * k, coarse_nodes + k * TILE)
        col_tables[j] = table(jnp.where(col_side == 1, nodes, rotated))


def pair_kernel(
    starts, counts, with_features, index_ref, pert_ref, lane_ref, tiles, partner_ref, perts, *rest
):
    if with_features:
        features, rest = rest[0], rest[1:]
    _, row_given, row_kept, col_given, col_kept, row_tables, col_tables, rows = rest
    tiles_col = col_tables.shape[0]
    step = pl.program_id(0)
    row_steps = counts[0] // STEP
    pert_count = pert_ref.shape[0]
    first = jnp.where(
        step < row_steps, starts[0] + step * STEP, starts[1] + (step - row_steps) * STEP
    )

    @pl.when(step == 0)
    def _():
        build_tables(partner_ref, row_tables, col_tables)

    hits = sum(
        ((pert_ref[p] >= first) & (pert_ref[p] < first + STEP)).astype(jnp.int32)
        for p in range(pert_count)
    )

    @pl.when(hits > 0)
    def _():
        for t in range(STEP):
            found = sum((pert_ref[p] == first + t).astype(jnp.int32) for p in range(pert_count))

            @pl.when(found > 0)
            def _():
                total = tiles[t].astype(F32)
                for p in range(pert_count):
                    total = total + jnp.where(pert_ref[p] == first + t, perts[p].astype(F32), 0.0)
                tiles[t] = total.astype(BF16)

    def put(t, both, given, kept, row_first):
        cross = both[:HALF, HALF:], both[HALF:, :HALF]
        given[0, t] = both[:HALF, :HALF]
        given[1, t] = cross[0 if row_first else 1]
        kept[0, t] = cross[1 if row_first else 0]
        kept[1, t] = both[HALF:, HALF:]

    def compute(given, kept, row_first):
        for t in range(STEP):
            i = lax.div(index_ref[first + t], tiles_col)
            rows[t] = jnp.dot(row_tables[i], tiles[t], preferred_element_type=F32).astype(BF16)
        for t in range(STEP):
            j = lax.rem(index_ref[first + t], tiles_col)
            both = jnp.dot(rows[t], col_tables[j], preferred_element_type=F32).astype(BF16)
            put(t, both, given, kept, row_first)

    @pl.when(step < row_steps)
    def _():
        compute(row_given, row_kept, True)
        if with_features:
            for t in range(features.shape[0]):
                table = row_tables[lane_ref[0] * features.shape[0] + t]
                both = jnp.dot(table, features[t], preferred_element_type=F32).astype(BF16)
                put(STEP + t, both, row_given, row_kept, True)

    @pl.when(step >= row_steps)
    def _():
        compute(col_given, col_kept, False)


def pair_tiles(
    starts, counts, index, pert_slot, lane, tile_values, partner, pert_values, features, sizes, token
):
    tiles_row, tiles_col = sizes
    row_steps, col_steps = counts[0] // STEP, counts[1] // STEP
    row_block, col_block = starts[0] // STEP, starts[1] // STEP
    with_features = features is not None
    extra = features.shape[0] // LANES if with_features else 0

    def tile_map(s, *_):
        return (jnp.where(s < row_steps, row_block + s, col_block + s - row_steps), 0, 0)

    shapes = [
        jax.ShapeDtypeStruct((2, count, HALF, HALF), BF16)
        for count in (counts[0] + extra,) * 2 + (counts[1],) * 2
    ]
    if with_features:
        row_out = full(shapes[0].shape)
    else:
        row_out = pl.BlockSpec(
            (2, STEP, HALF, HALF), lambda s, *_: (0, jnp.minimum(s, row_steps - 1), 0, 0)
        )
    col_out = pl.BlockSpec(
        (2, STEP, HALF, HALF), lambda s, *_: (0, jnp.maximum(s - row_steps, 0), 0, 0)
    )
    in_specs = [
        pl.BlockSpec((STEP, TILE, TILE), tile_map),
        full(partner.shape),
        full(pert_values.shape),
    ]
    operands = [tile_values, partner, pert_values]
    if with_features:
        in_specs.append(
            pl.BlockSpec((extra,) + features.shape[1:], lambda s, a, b, lane: (lane[0], 0, 0))
        )
        operands.append(features)
    return pl.pallas_call(
        functools.partial(pair_kernel, starts, counts, with_features),
        out_shape=shapes,
        grid_spec=pltpu.PrefetchScalarGridSpec(
            num_scalar_prefetch=3,
            grid=(row_steps + col_steps,),
            in_specs=in_specs + [ANYWHERE],
            out_specs=[row_out, row_out, col_out, col_out],
            scratch_shapes=[
                pltpu.VMEM((tiles_row, TILE, TILE), BF16),
                pltpu.VMEM((tiles_col, TILE, TILE), BF16),
                pltpu.VMEM((STEP, TILE, TILE), BF16),
            ],
        ),
        compiler_params=PARAMS,
        name="pair_tiles",
    )(index, pert_slot, lane, *operands, token)


def sum_kernel(bounds, tiles_col, index_ref, *rest):
    pieces, sums, total = rest[:-2], rest[-2], rest[-1]
    step = pl.program_id(0)

    @pl.when(step == 0)
    def _():
        total[...] = jnp.zeros_like(total)

    for number, (begin, steps, start, row_first) in enumerate(bounds):
        given, kept = pieces[2 * number], pieces[2 * number + 1]

        @pl.when((step >= begin) & (step < begin + steps))
        def _():
            for t in range(STEP):
                i = lax.div(index_ref[start + (step - begin) * STEP + t], tiles_col)
                cross = given[1, t].astype(F32), kept[0, t].astype(F32)
                given_part, kept_part = cross if row_first else cross[::-1]
                total[0, i] += given[0, t].astype(F32) + given_part
                total[1, i] += kept[1, t].astype(F32) + kept_part

    @pl.when(step == pl.num_programs(0) - 1)
    def _():
        row_side = position()[0]
        for i in range(total.shape[1]):
            given_line = jnp.sum(total[0, i].T, axis=0, keepdims=True)
            kept_line = jnp.sum(total[1, i].T, axis=0, keepdims=True)
            sums[i : i + 1, :HALF] = jnp.where(row_side == 1, given_line, kept_line)
            sums[i : i + 1, HALF:] = jnp.where(row_side == 1, kept_line, given_line)


def sum_rows(pieces, index, sizes):
    tiles_row, tiles_col = sizes
    bounds, specs, operands = [], [], []
    begin = 0
    for piece in pieces:
        steps = piece["count"] // STEP

        def block_map(s, *_, begin=begin, steps=steps):
            return (0, jnp.clip(s - begin, 0, steps - 1), 0, 0)

        specs += [pl.BlockSpec((2, STEP, HALF, HALF), block_map)] * 2
        operands += [piece["given"], piece["kept"]]
        bounds.append((begin, steps, piece["start"], piece["row_first"]))
        begin += steps
    return pl.pallas_call(
        functools.partial(sum_kernel, bounds, tiles_col),
        out_shape=jax.ShapeDtypeStruct((tiles_row, TILE), F32),
        grid_spec=pltpu.PrefetchScalarGridSpec(
            num_scalar_prefetch=1,
            grid=(begin,),
            in_specs=specs,
            out_specs=full((tiles_row, TILE)),
            scratch_shapes=[pltpu.VMEM((2, tiles_row, HALF, HALF), F32)],
        ),
        compiler_params=PARAMS,
        name="sum_rows",
    )(index, *operands)


def line_kernel(spread, _, out):
    line = jnp.sum(spread[...], axis=0, keepdims=True)
    out[...] = jnp.broadcast_to(line, out.shape)


def line_copies(spread, devices, token):
    return pl.pallas_call(
        line_kernel,
        out_shape=jax.ShapeDtypeStruct((devices, TILE), F32),
        in_specs=[pl.BlockSpec(memory_space=pltpu.VMEM), ANYWHERE],
        out_specs=pl.BlockSpec(memory_space=pltpu.VMEM),
        compiler_params=PARAMS,
        name="line_copies",
    )(spread, token)


def forward_kernel(steps, *refs):
    row_kept, row_came, col_kept, col_came = refs[:4]
    row_given, col_given = refs[-2:]
    step = pl.program_id(0)

    def both(kept, came, given):
        given[...] = (kept[0].astype(F32) + came[0].astype(F32)).astype(BF16)

    pl.when(step < steps[0])(lambda: both(row_kept, row_came, row_given))
    pl.when(step < steps[1])(lambda: both(col_kept, col_came, col_given))


def quadrant(which, steps):
    return pl.BlockSpec(
        (1, STEP, HALF, HALF), lambda s, *_: (which, jnp.minimum(s, steps - 1), 0, 0)
    )


def plain(steps):
    return pl.BlockSpec((STEP, HALF, HALF), lambda s, *_: (jnp.minimum(s, steps - 1), 0, 0))


def forward(pair, tokens):
    steps = [piece["count"] // STEP for piece in pair]
    operands = [piece[key] for piece in pair for key in ("kept", "came")]
    return pl.pallas_call(
        functools.partial(forward_kernel, steps),
        out_shape=[jax.ShapeDtypeStruct((piece["count"], HALF, HALF), BF16) for piece in pair],
        grid=(max(steps),),
        in_specs=[quadrant(0, steps[k // 2]) for k in range(4)] + [ANYWHERE] * len(tokens),
        out_specs=[plain(steps[0]), plain(steps[1])],
        compiler_params=PARAMS,
        name="forward",
    )(*operands, *tokens)


def zero_kernel(_, out):
    out[...] = jnp.zeros_like(out)


def zero_buffer(count, token):
    return pl.pallas_call(
        zero_kernel,
        out_shape=jax.ShapeDtypeStruct((count, HALF, HALF), BF16),
        grid=(count // 64,),
        in_specs=[ANYWHERE],
        out_specs=pl.BlockSpec((64, HALF, HALF), lambda s: (s, 0, 0)),
        compiler_params=PARAMS,
        name="zero_buffer",
    )(token)


def store_roots(raw, scale):
    half = raw.shape[0] // 2
    total = raw[:half] + raw[half:]
    roots = 1.0 / jnp.sqrt(1.0 + total / (total.shape[0] * total.shape[1]))
    scale[0] = roots[:, :HALF]
    scale[1] = roots[:, HALF:]


def upright(line):
    return jnp.broadcast_to(line, (HALF, HALF)).T


def finish_kernel(starts, counts, index_ref, place_ref, *refs):
    pieces, raw = (refs[0:3], refs[3:6]), refs[6]
    out, scale, row_scale, col_scale, done, sem = refs[-6:]
    tiles_row = row_scale.shape[0]
    tiles_col = col_scale.shape[0]
    step = pl.program_id(0)

    @pl.when(step == 0)
    def _():
        row_side, row_group, col_side, col_group = position()
        store_roots(raw, scale)
        for i in range(tiles_row):
            row_scale[i] = upright(scale[row_side, pl.ds(row_group * tiles_row + i, 1), :])
        for j in range(tiles_col):
            line = scale[col_side, pl.ds(col_group * tiles_col + j, 1), :]
            col_scale[j] = jnp.broadcast_to(line, (8, HALF))

    for number in range(2):
        kept, came, last = pieces[number]
        base = number * counts[0]

        @pl.when(step < counts[number] // STEP)
        def _():
            for t in range(STEP):
                m = step * STEP + t
                n = starts[number] + m
                i = lax.div(index_ref[n], tiles_col)
                j = lax.rem(index_ref[n], tiles_col)
                total = kept[0, t].astype(F32) + came[0, t].astype(F32) + last[t].astype(F32)
                done[base + m] = (total * row_scale[i] * col_scale[j, 0:1]).astype(BF16)
                pltpu.make_async_copy(done.at[base + m], out.at[place_ref[n]], sem).start()

    @pl.when(step == pl.num_programs(0) - 1)
    def _():
        pltpu.make_async_copy(done, out.at[pl.ds(0, done.shape[0])], sem).wait()


def finish(pair, index, place, raw, buffer, sizes, token):
    tiles_row, tiles_col = sizes
    starts = [piece["start"] for piece in pair]
    counts = [piece["count"] for piece in pair]
    specs, operands = [], []
    for piece in pair:
        steps = piece["count"] // STEP
        specs += [quadrant(1, steps), quadrant(1, steps), plain(steps)]
        operands += [piece["kept"], piece["came"], piece["last"]]
    return pl.pallas_call(
        functools.partial(finish_kernel, starts, counts),
        out_shape=jax.ShapeDtypeStruct(buffer.shape, BF16),
        grid_spec=pltpu.PrefetchScalarGridSpec(
            num_scalar_prefetch=2,
            grid=(max(counts) // STEP,),
            in_specs=specs + [full(raw.shape), ANYWHERE, ANYWHERE],
            out_specs=ANYWHERE,
            scratch_shapes=[
                pltpu.VMEM((2, raw.shape[0] // 2, HALF), F32),
                pltpu.VMEM((tiles_row, HALF, HALF), F32),
                pltpu.VMEM((tiles_col, 8, HALF), F32),
                pltpu.VMEM((sum(counts), HALF, HALF), BF16),
                pltpu.SemaphoreType.DMA,
            ],
        ),
        input_output_aliases={9: 0},
        compiler_params=PARAMS,
        name="finish",
    )(index, place, *operands, raw, buffer, token)


def join_kernel(tiles_row, lane_ref, kept, came, weight, raw, _, out, scale):
    row_side, row_group, _, _ = position()
    part = out.shape[0]
    store_roots(raw, scale)
    for t in range(part):
        merged = [
            (kept[h, t].astype(F32) + came[h, t].astype(F32)).astype(BF16) for h in range(2)
        ]
        joined = jnp.dot(
            jnp.concatenate(merged, axis=1), weight[...], preferred_element_type=F32
        )
        k = row_group * tiles_row + lane_ref[0] * part + t
        column = upright(scale[row_side, pl.ds(k, 1), :])
        out[t] = (joined * jnp.concatenate([column] * 2, axis=1)).astype(BF16)


def join_features(lane, piece, weight, raw, tiles_row, token):
    part = tiles_row // LANES
    block = pl.BlockSpec((2, part, HALF, HALF), lambda s, *_: (0, piece["count"] // part, 0, 0))
    shape = (part, HALF, weight.shape[1])
    return pl.pallas_call(
        functools.partial(join_kernel, tiles_row),
        out_shape=jax.ShapeDtypeStruct(shape, BF16),
        grid_spec=pltpu.PrefetchScalarGridSpec(
            num_scalar_prefetch=1,
            grid=(1,),
            in_specs=[block, block, full(weight.shape), full(raw.shape), ANYWHERE],
            out_specs=full(shape),
            scratch_shapes=[pltpu.VMEM((2, raw.shape[0] // 2, HALF), F32)],
        ),
        compiler_params=PARAMS,
        name="join_features",
    )(lane, piece["kept"], piece["came"], weight, raw, token)


def copy_kernel(parts, source, out, sem):
    size = source.shape[0] // parts

    def move(k):
        window = pl.ds(k * size, size)
        return pltpu.make_async_copy(source.at[window], out.at[window], sem.at[k])

    for k in range(parts):
        move(k).start()
    for k in range(parts):
        move(k).wait()


def copied(source):
    parts = 16
    return pl.pallas_call(
        functools.partial(copy_kernel, parts),
        out_shape=jax.ShapeDtypeStruct(source.shape, source.dtype),
        in_specs=[ANYWHERE],
        out_specs=ANYWHERE,
        scratch_shapes=[pltpu.SemaphoreType.DMA((parts,))],
        compiler_params=pltpu.CompilerParams(vmem_limit_bytes=1 << 20),
        name="copied",
    )(source)


def level(features, join_weight, partner, tile_index, tile_values, pert_slot, pert_values, routes):
    row_count = lax.axis_size("row")
    col_count = lax.axis_size("col")
    devices = row_count * col_count
    masks = ("row", row_count // 2), ("col", col_count // 2)
    slot_count = tile_values.shape[0]
    width = features.shape[1]
    tiles_row = features.shape[0] // TILE
    tiles_col = partner.shape[0] // TILE // col_count
    sizes = tiles_row, tiles_col
    capacity = routes.shape[1]
    part = tiles_row // LANES
    chunks = len(CHUNKS)
    lane = (lax.axis_index("col") % LANES).reshape(1)
    partner = partner.reshape(-1, HALF)
    feature_tiles = features.reshape(tiles_row, TILE, width)

    starts = [0, ROW_FIRST]
    token = pert_values
    pairs = []
    for chunk in range(chunks):
        counts = CHUNKS[chunk]
        row_given, row_kept, col_given, col_kept = pair_tiles(
            tuple(starts), counts, tile_index, pert_slot, lane, tile_values, partner,
            pert_values, feature_tiles if chunk == 0 else None, sizes, token,
        )
        token = col_kept
        pair = []
        for kind, (given, kept) in enumerate(((row_given, row_kept), (col_given, col_kept))):
            came = flipped(given, *masks[kind])
            pair.append(
                dict(
                    row_first=kind == 0, start=starts[kind], count=counts[kind],
                    given=given, kept=kept, came=came,
                )
            )
            starts[kind] += counts[kind]
        pairs.append(pair)

    own = sum_rows([piece for pair in pairs for piece in pair], tile_index, sizes)
    spread = lax.all_to_all(own, "col", split_axis=0, concat_axis=0, tiled=True)

    targets = routes[:, 0]
    order = jnp.arange(slot_count, dtype=jnp.int32)
    same = (targets[:, None] == targets[None, :]) & (order[None, :] < order[:, None])
    place = targets * capacity + jnp.sum(same.astype(jnp.int32), axis=1)

    buffer = zero_buffer(devices * capacity, own)
    lines = line_copies(spread, devices, buffer)
    raw = lax.all_to_all(lines, ("row", "col"), split_axis=0, concat_axis=0, tiled=True)
    token = lines
    for pair in pairs:
        given = forward(pair, [token])
        token = given[0]
        for kind in range(2):
            pair[kind]["last"] = flipped(given[kind], *masks[1 - kind])

    def finished(chunk, buffer, token):
        return finish(pairs[chunk], tile_index, place, raw, buffer, sizes, token)

    buffer = finished(0, buffer, token)
    joined = join_features(lane, pairs[0][0], join_weight, raw, tiles_row, buffer)
    buffer = finished(1, buffer, joined)
    parts = jnp.zeros((LANES, part, HALF, width), BF16)
    for shift in range(LANES):
        shared = joined
        if shift > 0:
            ring = [
                (source, source // LANES * LANES + (source + shift) % LANES)
                for source in range(col_count)
            ]
            shared = lax.ppermute(joined, "col", ring)
        parts = lax.dynamic_update_slice(
            parts, shared[None], ((lane[0] - shift) % LANES, 0, 0, 0)
        )
    buffer = finished(2, buffer, parts)
    coarse_features = parts.reshape(tiles_row * HALF, width)
    arrived = lax.all_to_all(buffer, ("row", "col"), split_axis=0, concat_axis=0, tiled=True)
    return (coarse_features, copied(arrived))


def solution(mesh):
    both = P(("row", "col"))
    placed = (
        P("row", None),
        P(),
        P(),
        both,
        P(("row", "col"), None, None),
        both,
        P(("row", "col"), None, None),
        P(("row", "col"), None),
    )
    return jax.shard_map(
        level,
        mesh=mesh,
        in_specs=placed,
        out_specs=(P("row", None), P(("row", "col"), None, None)),
        check_vma=False,
    )
```

```python
import functools

import jax
import jax.numpy as jnp
from jax import lax
from jax.experimental import pallas as pl
from jax.experimental.pallas import tpu as pltpu
from jax.sharding import PartitionSpec as P


TILE = 256
HALF = 128
STEP = 8
LANES = 4
ROW_FIRST = 48
CHUNKS = (8, 16), (24, 24), (16, 16)
SPLITS = 1, 2, 2
BF16 = jnp.bfloat16
F32 = jnp.float32
PARAMS = pltpu.CompilerParams(vmem_limit_bytes=66_500_000)
ANYWHERE = pl.BlockSpec(memory_space=pl.ANY)


def flipped(value, axis, mask):
    pairs = [(source, source ^ mask) for source in range(lax.axis_size(axis))]
    return lax.ppermute(value, axis, pairs)


def full(shape):
    return pl.BlockSpec(shape, lambda *_: (0,) * len(shape))


def iota(shape, axis):
    return lax.broadcasted_iota(jnp.int32, shape, axis)


def position():
    row_half = lax.axis_size("row") // 2
    col_half = lax.axis_size("col") // 2
    row_index = lax.axis_index("row")
    col_index = lax.axis_index("col")
    return (
        lax.div(row_index, row_half),
        lax.rem(row_index, row_half),
        lax.div(col_index, col_half),
        lax.rem(col_index, col_half),
    )


def build_tables(partner_ref, row_tables, col_tables):
    row_side, row_group, col_side, col_group = position()
    tiles_row = row_tables.shape[0]
    tiles_col = col_tables.shape[0]
    coarse_nodes = partner_ref.shape[0] * HALF // 2
    rotated = (iota((1, TILE), 1) + HALF) & (TILE - 1)
    level = iota((TILE, TILE), 0).astype(F32).astype(BF16)

    def vector(start, shift):
        first = partner_ref[pl.ds(start, 1), :]
        second = partner_ref[pl.ds(start + 1, 1), :]
        return jnp.concatenate([first, second], axis=1) - shift

    def table(values):
        line = values.astype(F32).astype(BF16)
        same = jnp.broadcast_to(line, (TILE, TILE)) == level
        return jnp.where(same, jnp.ones((), BF16), jnp.zeros((), BF16))

    for i in range(tiles_row):
        k = row_group * tiles_row + i
        slots = vector(coarse_nodes // HALF + 2 * k, k * TILE)
        row_tables[i] = table(jnp.where(row_side == 1, slots, rotated))
    for j in range(tiles_col):
        k = col_group * tiles_col + j
        nodes = vector(2 * k, coarse_nodes + k * TILE)
        col_tables[j] = table(jnp.where(col_side == 1, nodes, rotated))


def pair_kernel(
    starts, counts, with_features, index_ref, pert_ref, lane_ref, tiles, partner_ref, perts, *rest
):
    if with_features:
        features, rest = rest[0], rest[1:]
    _, row_given, row_kept, col_given, col_kept, row_tables, col_tables, rows = rest
    tiles_col = col_tables.shape[0]
    step = pl.program_id(0)
    row_steps = counts[0] // STEP
    pert_count = pert_ref.shape[0]
    first = jnp.where(
        step < row_steps, starts[0] + step * STEP, starts[1] + (step - row_steps) * STEP
    )

    @pl.when(step == 0)
    def _():
        build_tables(partner_ref, row_tables, col_tables)

    hits = sum(
        ((pert_ref[p] >= first) & (pert_ref[p] < first + STEP)).astype(jnp.int32)
        for p in range(pert_count)
    )

    @pl.when(hits > 0)
    def _():
        for t in range(STEP):
            found = sum((pert_ref[p] == first + t).astype(jnp.int32) for p in range(pert_count))

            @pl.when(found > 0)
            def _():
                total = tiles[t].astype(F32)
                for p in range(pert_count):
                    total = total + jnp.where(pert_ref[p] == first + t, perts[p].astype(F32), 0.0)
                tiles[t] = total.astype(BF16)

    def put(t, both, given, kept, row_first):
        cross = both[:HALF, HALF:], both[HALF:, :HALF]
        given[0, t] = both[:HALF, :HALF]
        given[1, t] = cross[0 if row_first else 1]
        kept[0, t] = cross[1 if row_first else 0]
        kept[1, t] = both[HALF:, HALF:]

    def compute(given, kept, row_first):
        for t in range(STEP):
            i = lax.div(index_ref[first + t], tiles_col)
            rows[t] = jnp.dot(row_tables[i], tiles[t], preferred_element_type=F32).astype(BF16)
        for t in range(STEP):
            j = lax.rem(index_ref[first + t], tiles_col)
            both = jnp.dot(rows[t], col_tables[j], preferred_element_type=F32).astype(BF16)
            put(t, both, given, kept, row_first)

    @pl.when(step < row_steps)
    def _():
        compute(row_given, row_kept, True)
        if with_features:
            for t in range(features.shape[0]):
                table = row_tables[lane_ref[0] * features.shape[0] + t]
                both = jnp.dot(table, features[t], preferred_element_type=F32).astype(BF16)
                put(STEP + t, both, row_given, row_kept, True)

    @pl.when(step >= row_steps)
    def _():
        compute(col_given, col_kept, False)


def pair_tiles(
    starts, counts, index, pert_slot, lane, tile_values, partner, pert_values, features, sizes, token
):
    tiles_row, tiles_col = sizes
    row_steps, col_steps = counts[0] // STEP, counts[1] // STEP
    row_block, col_block = starts[0] // STEP, starts[1] // STEP
    with_features = features is not None
    extra = features.shape[0] // LANES if with_features else 0

    def tile_map(s, *_):
        return (jnp.where(s < row_steps, row_block + s, col_block + s - row_steps), 0, 0)

    shapes = [
        jax.ShapeDtypeStruct((2, count, HALF, HALF), BF16)
        for count in (counts[0] + extra,) * 2 + (counts[1],) * 2
    ]
    if with_features:
        row_out = full(shapes[0].shape)
    else:
        row_out = pl.BlockSpec(
            (2, STEP, HALF, HALF), lambda s, *_: (0, jnp.minimum(s, row_steps - 1), 0, 0)
        )
    col_out = pl.BlockSpec(
        (2, STEP, HALF, HALF), lambda s, *_: (0, jnp.maximum(s - row_steps, 0), 0, 0)
    )
    in_specs = [
        pl.BlockSpec((STEP, TILE, TILE), tile_map),
        full(partner.shape),
        full(pert_values.shape),
    ]
    operands = [tile_values, partner, pert_values]
    if with_features:
        in_specs.append(
            pl.BlockSpec((extra,) + features.shape[1:], lambda s, a, b, lane: (lane[0], 0, 0))
        )
        operands.append(features)
    return pl.pallas_call(
        functools.partial(pair_kernel, starts, counts, with_features),
        out_shape=shapes,
        grid_spec=pltpu.PrefetchScalarGridSpec(
            num_scalar_prefetch=3,
            grid=(row_steps + col_steps,),
            in_specs=in_specs + [ANYWHERE],
            out_specs=[row_out, row_out, col_out, col_out],
            scratch_shapes=[
                pltpu.VMEM((tiles_row, TILE, TILE), BF16),
                pltpu.VMEM((tiles_col, TILE, TILE), BF16),
                pltpu.VMEM((STEP, TILE, TILE), BF16),
            ],
        ),
        compiler_params=PARAMS,
        name="pair_tiles",
    )(index, pert_slot, lane, *operands, token)


def sum_kernel(bounds, tiles_col, index_ref, *rest):
    pieces, sums, total = rest[:-2], rest[-2], rest[-1]
    step = pl.program_id(0)

    @pl.when(step == 0)
    def _():
        total[...] = jnp.zeros_like(total)

    for number, (begin, steps, start, row_first) in enumerate(bounds):
        given, kept = pieces[2 * number], pieces[2 * number + 1]

        @pl.when((step >= begin) & (step < begin + steps))
        def _():
            for t in range(STEP):
                i = lax.div(index_ref[start + (step - begin) * STEP + t], tiles_col)
                cross = given[1, t].astype(F32), kept[0, t].astype(F32)
                given_part, kept_part = cross if row_first else cross[::-1]
                total[0, i] += given[0, t].astype(F32) + given_part
                total[1, i] += kept[1, t].astype(F32) + kept_part

    @pl.when(step == pl.num_programs(0) - 1)
    def _():
        row_side = position()[0]
        for i in range(total.shape[1]):
            given_line = jnp.sum(total[0, i].T, axis=0, keepdims=True)
            kept_line = jnp.sum(total[1, i].T, axis=0, keepdims=True)
            sums[i : i + 1, :HALF] = jnp.where(row_side == 1, given_line, kept_line)
            sums[i : i + 1, HALF:] = jnp.where(row_side == 1, kept_line, given_line)


def sum_rows(pieces, index, sizes):
    tiles_row, tiles_col = sizes
    bounds, specs, operands = [], [], []
    begin = 0
    for piece in pieces:
        steps = piece["count"] // STEP

        def block_map(s, *_, begin=begin, steps=steps):
            return (0, jnp.clip(s - begin, 0, steps - 1), 0, 0)

        specs += [pl.BlockSpec((2, STEP, HALF, HALF), block_map)] * 2
        operands += [piece["given"], piece["kept"]]
        bounds.append((begin, steps, piece["start"], piece["row_first"]))
        begin += steps
    return pl.pallas_call(
        functools.partial(sum_kernel, bounds, tiles_col),
        out_shape=jax.ShapeDtypeStruct((tiles_row, TILE), F32),
        grid_spec=pltpu.PrefetchScalarGridSpec(
            num_scalar_prefetch=1,
            grid=(begin,),
            in_specs=specs,
            out_specs=full((tiles_row, TILE)),
            scratch_shapes=[pltpu.VMEM((2, tiles_row, HALF, HALF), F32)],
        ),
        compiler_params=PARAMS,
        name="sum_rows",
    )(index, *operands)


def line_kernel(spread, _, out):
    line = jnp.sum(spread[...], axis=0, keepdims=True)
    out[...] = jnp.broadcast_to(line, out.shape)


def line_copies(spread, devices, token):
    return pl.pallas_call(
        line_kernel,
        out_shape=jax.ShapeDtypeStruct((devices, TILE), F32),
        in_specs=[pl.BlockSpec(memory_space=pltpu.VMEM), ANYWHERE],
        out_specs=pl.BlockSpec(memory_space=pltpu.VMEM),
        compiler_params=PARAMS,
        name="line_copies",
    )(spread, token)


def forward_kernel(steps, parts, *refs):
    row_kept, row_came, col_kept, col_came = refs[:4]
    row_given, col_given = refs[-2 * parts : -parts], refs[-parts:]
    step = pl.program_id(0)
    size = HALF // parts

    def both(kept, came, given):
        total = (kept[0].astype(F32) + came[0].astype(F32)).astype(BF16)
        for h in range(parts):
            given[h][...] = total[:, h * size : (h + 1) * size]

    pl.when(step < steps[0])(lambda: both(row_kept, row_came, row_given))
    pl.when(step < steps[1])(lambda: both(col_kept, col_came, col_given))


def quadrant(which, steps, size=HALF, h=0):
    return pl.BlockSpec(
        (1, STEP, size, HALF), lambda s, *_: (which, jnp.minimum(s, steps - 1), h, 0)
    )


def plain(steps, size=HALF, h=0):
    return pl.BlockSpec((STEP, size, HALF), lambda s, *_: (jnp.minimum(s, steps - 1), h, 0))


def forward(pair, parts, tokens):
    steps = [piece["count"] // STEP for piece in pair]
    operands = [piece[key] for piece in pair for key in ("kept", "came")]
    size = HALF // parts
    return pl.pallas_call(
        functools.partial(forward_kernel, steps, parts),
        out_shape=[
            jax.ShapeDtypeStruct((piece["count"], size, HALF), BF16)
            for piece in pair
            for _ in range(parts)
        ],
        grid=(max(steps),),
        in_specs=[quadrant(0, steps[k // 2]) for k in range(4)] + [ANYWHERE] * len(tokens),
        out_specs=[plain(steps[k], size) for k in range(2) for _ in range(parts)],
        compiler_params=PARAMS,
        name="forward",
    )(*operands, *tokens)


def zero_kernel(_, *outs):
    for out in outs:
        out[...] = jnp.zeros_like(out)


def zero_buffers(count, token):
    block = pl.BlockSpec((64, HALF // 2, HALF), lambda s: (s, 0, 0))
    return pl.pallas_call(
        zero_kernel,
        out_shape=[jax.ShapeDtypeStruct((count, HALF // 2, HALF), BF16)] * 2,
        grid=(count // 64,),
        in_specs=[ANYWHERE],
        out_specs=[block, block],
        compiler_params=PARAMS,
        name="zero_buffers",
    )(token)


def store_roots(raw, scale):
    half = raw.shape[0] // 2
    total = raw[:half] + raw[half:]
    roots = 1.0 / jnp.sqrt(1.0 + total / (total.shape[0] * total.shape[1]))
    scale[0] = roots[:, :HALF]
    scale[1] = roots[:, HALF:]


def upright(line):
    return jnp.broadcast_to(line, (HALF, HALF)).T


def finish_kernel(starts, counts, h, index_ref, place_ref, *refs):
    total_pieces = len(starts)
    raw = refs[3 * total_pieces]
    out, scale, row_scale, col_scale, done, sem = refs[-6:]
    tiles_row, size, _ = row_scale.shape
    tiles_col = col_scale.shape[0]
    step = pl.program_id(0)

    @pl.when(step == 0)
    def _():
        row_side, row_group, col_side, col_group = position()
        store_roots(raw, scale)
        for i in range(tiles_row):
            column = upright(scale[row_side, pl.ds(row_group * tiles_row + i, 1), :])
            row_scale[i] = column[h * size : (h + 1) * size]
        for j in range(tiles_col):
            line = scale[col_side, pl.ds(col_group * tiles_col + j, 1), :]
            col_scale[j] = jnp.broadcast_to(line, (8, HALF))

    base = 0
    for number in range(total_pieces):
        kept, came, last = refs[3 * number : 3 * number + 3]

        @pl.when(step < counts[number] // STEP)
        def _(kept=kept, came=came, last=last, base=base, start=starts[number]):
            for t in range(STEP):
                m = step * STEP + t
                i = lax.div(index_ref[start + m], tiles_col)
                j = lax.rem(index_ref[start + m], tiles_col)
                total = kept[0, t].astype(F32) + came[0, t].astype(F32) + last[t].astype(F32)
                done[base + m] = (total * row_scale[i] * col_scale[j, 0:1]).astype(BF16)
                target = out.at[place_ref[start + m]]
                pltpu.make_async_copy(done.at[base + m], target, sem).start()

        base += counts[number]

    @pl.when(step == pl.num_programs(0) - 1)
    def _():
        pltpu.make_async_copy(done, out.at[pl.ds(0, done.shape[0])], sem).wait()


def finish(pieces, h, index, place, raw, buffer, sizes, token):
    tiles_row, tiles_col = sizes
    size = buffer.shape[1]
    starts = [piece["start"] for piece in pieces]
    counts = [piece["count"] for piece in pieces]
    specs, operands = [], []
    for piece in pieces:
        steps = piece["count"] // STEP
        split = len(piece["last"]) > 1
        specs += [quadrant(1, steps, size, h)] * 2 + [plain(steps, size, 0 if split else h)]
        operands += [piece["kept"], piece["came"], piece["last"][h if split else 0]]
    return pl.pallas_call(
        functools.partial(finish_kernel, starts, counts, h),
        out_shape=jax.ShapeDtypeStruct(buffer.shape, BF16),
        grid_spec=pltpu.PrefetchScalarGridSpec(
            num_scalar_prefetch=2,
            grid=(max(counts) // STEP,),
            in_specs=specs + [full(raw.shape), ANYWHERE, ANYWHERE],
            out_specs=ANYWHERE,
            scratch_shapes=[
                pltpu.VMEM((2, raw.shape[0] // 2, HALF), F32),
                pltpu.VMEM((tiles_row, size, HALF), F32),
                pltpu.VMEM((tiles_col, 8, HALF), F32),
                pltpu.VMEM((sum(counts), size, HALF), BF16),
                pltpu.SemaphoreType.DMA,
            ],
        ),
        input_output_aliases={3 + len(operands): 0},
        compiler_params=PARAMS,
        name="finish",
    )(index, place, *operands, raw, buffer, token)


def join_kernel(tiles_row, lane_ref, kept, came, weight, raw, _, out, scale):
    row_side, row_group, _, _ = position()
    part = out.shape[0]
    store_roots(raw, scale)
    for t in range(part):
        merged = [
            (kept[h, t].astype(F32) + came[h, t].astype(F32)).astype(BF16) for h in range(2)
        ]
        joined = jnp.dot(
            jnp.concatenate(merged, axis=1), weight[...], preferred_element_type=F32
        )
        k = row_group * tiles_row + lane_ref[0] * part + t
        column = upright(scale[row_side, pl.ds(k, 1), :])
        out[t] = (joined * jnp.concatenate([column] * 2, axis=1)).astype(BF16)


def join_features(lane, piece, weight, raw, tiles_row, token):
    part = tiles_row // LANES
    block = pl.BlockSpec((2, part, HALF, HALF), lambda s, *_: (0, piece["count"] // part, 0, 0))
    shape = (part, HALF, weight.shape[1])
    return pl.pallas_call(
        functools.partial(join_kernel, tiles_row),
        out_shape=jax.ShapeDtypeStruct(shape, BF16),
        grid_spec=pltpu.PrefetchScalarGridSpec(
            num_scalar_prefetch=1,
            grid=(1,),
            in_specs=[block, block, full(weight.shape), full(raw.shape), ANYWHERE],
            out_specs=full(shape),
            scratch_shapes=[pltpu.VMEM((2, raw.shape[0] // 2, HALF), F32)],
        ),
        compiler_params=PARAMS,
        name="join_features",
    )(lane, piece["kept"], piece["came"], weight, raw, token)


def assemble_kernel(*refs):
    shared, out = refs[:LANES], refs[-1]
    part = shared[0].shape[0]
    lane = lax.rem(lax.axis_index("col"), LANES)
    for shift in range(LANES):
        owner = lax.rem(lane + LANES - shift, LANES)
        out[pl.ds(owner * part, part)] = shared[shift][...]


def assemble(shared, token):
    part = shared[0].shape[0]
    inner = shared[0].shape[1:]
    shape = (LANES * part,) + inner
    return pl.pallas_call(
        assemble_kernel,
        out_shape=jax.ShapeDtypeStruct(shape, BF16),
        grid=(1,),
        in_specs=[full((part,) + inner)] * LANES + [ANYWHERE],
        out_specs=full(shape),
        compiler_params=pltpu.CompilerParams(vmem_limit_bytes=8 << 20),
        name="assemble",
    )(*shared, token)


def copy_kernel(parts, h, source, *refs):
    out, sem = refs[-2:]
    count = source.shape[0] // parts
    size = source.shape[1]

    def move(k):
        window = pl.ds(k * count, count)
        target = out.at[window, pl.ds(h * size, size)]
        return pltpu.make_async_copy(source.at[window], target, sem.at[k])

    for k in range(parts):
        move(k).start()
    for k in range(parts):
        move(k).wait()


def copied(source, h, out):
    parts = 16
    shape = (source.shape[0], 2 * source.shape[1], source.shape[2])
    operands = [source] if out is None else [source, out]
    return pl.pallas_call(
        functools.partial(copy_kernel, parts, h),
        out_shape=jax.ShapeDtypeStruct(shape, source.dtype),
        in_specs=[ANYWHERE] * len(operands),
        out_specs=ANYWHERE,
        scratch_shapes=[pltpu.SemaphoreType.DMA((parts,))],
        input_output_aliases={} if out is None else {1: 0},
        compiler_params=pltpu.CompilerParams(vmem_limit_bytes=1 << 20),
        name="copied",
    )(*operands)


def level(features, join_weight, partner, tile_index, tile_values, pert_slot, pert_values, routes):
    row_count = lax.axis_size("row")
    col_count = lax.axis_size("col")
    devices = row_count * col_count
    masks = ("row", row_count // 2), ("col", col_count // 2)
    slot_count = tile_values.shape[0]
    width = features.shape[1]
    tiles_row = features.shape[0] // TILE
    tiles_col = partner.shape[0] // TILE // col_count
    sizes = tiles_row, tiles_col
    capacity = routes.shape[1]
    chunks = len(CHUNKS)
    lane = (lax.axis_index("col") % LANES).reshape(1)
    partner = partner.reshape(-1, HALF)
    feature_tiles = features.reshape(tiles_row, TILE, width)

    starts = [0, ROW_FIRST]
    token = pert_values
    pairs = []
    for chunk in range(chunks):
        counts = CHUNKS[chunk]
        row_given, row_kept, col_given, col_kept = pair_tiles(
            tuple(starts), counts, tile_index, pert_slot, lane, tile_values, partner,
            pert_values, feature_tiles if chunk == 0 else None, sizes, token,
        )
        token = col_kept
        pair = []
        for kind, (given, kept) in enumerate(((row_given, row_kept), (col_given, col_kept))):
            came = flipped(given, *masks[kind])
            pair.append(
                dict(
                    row_first=kind == 0, start=starts[kind], count=counts[kind],
                    given=given, kept=kept, came=came,
                )
            )
            starts[kind] += counts[kind]
        pairs.append(pair)

    own = sum_rows([piece for pair in pairs for piece in pair], tile_index, sizes)
    spread = lax.all_to_all(own, "col", split_axis=0, concat_axis=0, tiled=True)

    targets = routes[:, 0]
    order = jnp.arange(slot_count, dtype=jnp.int32)
    same = (targets[:, None] == targets[None, :]) & (order[None, :] < order[:, None])
    place = targets * capacity + jnp.sum(same.astype(jnp.int32), axis=1)

    buffers = list(zero_buffers(devices * capacity, own))
    token = buffers[0]
    for chunk, pair in enumerate(pairs):
        splits = SPLITS[chunk]
        given = forward(pair, splits, [token])
        token = given[0]
        for kind in range(2):
            pair[kind]["last"] = []
            for h in range(splits):
                last = flipped(given[kind * splits + h], *masks[1 - kind])
                pair[kind]["last"].append(last)
        if chunk == 0:
            token = line_copies(spread, devices, token)
            raw = lax.all_to_all(token, ("row", "col"), split_axis=0, concat_axis=0, tiled=True)

    def finished(pieces, h, token):
        return finish(pieces, h, tile_index, place, raw, buffers[h], sizes, token)

    def delivered(h):
        return lax.all_to_all(buffers[h], ("row", "col"), split_axis=0, concat_axis=0, tiled=True)

    joined = join_features(lane, pairs[0][0], join_weight, raw, tiles_row, token)
    shared = [joined]
    for shift in range(1, LANES):
        ring = [
            (source, source // LANES * LANES + (source + shift) % LANES)
            for source in range(col_count)
        ]
        shared.append(lax.ppermute(joined, "col", ring))
    buffers[0] = finished(pairs[0] + pairs[1], 0, joined)
    buffers[0] = finished(pairs[2], 0, joined)
    buffers[1] = finished(pairs[0] + pairs[1] + pairs[2], 1, buffers[0])
    first = delivered(0)
    second = delivered(1)
    coarse_features = assemble(shared, buffers[1]).reshape(tiles_row * HALF, width)
    result = copied(first, 0, None)
    result = copied(second, 1, result)
    return (coarse_features, result)


def solution(mesh):
    both = P(("row", "col"))
    placed = (
        P("row", None),
        P(),
        P(),
        both,
        P(("row", "col"), None, None),
        both,
        P(("row", "col"), None, None),
        P(("row", "col"), None),
    )
    return jax.shard_map(
        level,
        mesh=mesh,
        in_specs=placed,
        out_specs=(P("row", None), P(("row", "col"), None, None)),
        check_vma=False,
    )
```

```python
import functools

import jax
import jax.numpy as jnp
from jax import lax
from jax.experimental import pallas as pl
from jax.experimental.pallas import tpu as pltpu
from jax.sharding import PartitionSpec as P


TILE = 256
HALF = 128
STEP = 8
LANES = 4
ROW_FIRST = 48
CHUNKS = (8, 16), (24, 24), (16, 16)
BF16 = jnp.bfloat16
F32 = jnp.float32
PARAMS = pltpu.CompilerParams(vmem_limit_bytes=66_500_000)
ANYWHERE = pl.BlockSpec(memory_space=pl.ANY)


def flipped(value, axis, mask):
    pairs = [(source, source ^ mask) for source in range(lax.axis_size(axis))]
    return lax.ppermute(value, axis, pairs)


def full(shape):
    return pl.BlockSpec(shape, lambda *_: (0,) * len(shape))


def iota(shape, axis):
    return lax.broadcasted_iota(jnp.int32, shape, axis)


def position():
    row_half = lax.axis_size("row") // 2
    col_half = lax.axis_size("col") // 2
    row_index = lax.axis_index("row")
    col_index = lax.axis_index("col")
    return (
        lax.div(row_index, row_half),
        lax.rem(row_index, row_half),
        lax.div(col_index, col_half),
        lax.rem(col_index, col_half),
    )


def build_tables(partner_ref, row_tables, col_tables):
    row_side, row_group, col_side, col_group = position()
    tiles_row = row_tables.shape[0]
    tiles_col = col_tables.shape[0]
    coarse_nodes = partner_ref.shape[0] * HALF // 2
    rotated = (iota((1, TILE), 1) + HALF) & (TILE - 1)
    level = iota((TILE, TILE), 0).astype(F32).astype(BF16)

    def vector(start, shift):
        first = partner_ref[pl.ds(start, 1), :]
        second = partner_ref[pl.ds(start + 1, 1), :]
        return jnp.concatenate([first, second], axis=1) - shift

    def table(values):
        line = values.astype(F32).astype(BF16)
        same = jnp.broadcast_to(line, (TILE, TILE)) == level
        return jnp.where(same, jnp.ones((), BF16), jnp.zeros((), BF16))

    for i in range(tiles_row):
        k = row_group * tiles_row + i
        slots = vector(coarse_nodes // HALF + 2 * k, k * TILE)
        row_tables[i] = table(jnp.where(row_side == 1, slots, rotated))
    for j in range(tiles_col):
        k = col_group * tiles_col + j
        nodes = vector(2 * k, coarse_nodes + k * TILE)
        col_tables[j] = table(jnp.where(col_side == 1, nodes, rotated))


def pair_kernel(
    starts, counts, with_features, index_ref, pert_ref, lane_ref, tiles, partner_ref, perts, *rest
):
    if with_features:
        features, rest = rest[0], rest[1:]
    _, row_given, row_kept, col_given, col_kept, row_tables, col_tables, rows = rest
    tiles_col = col_tables.shape[0]
    step = pl.program_id(0)
    row_steps = counts[0] // STEP
    pert_count = pert_ref.shape[0]
    first = jnp.where(
        step < row_steps, starts[0] + step * STEP, starts[1] + (step - row_steps) * STEP
    )

    @pl.when(step == 0)
    def _():
        build_tables(partner_ref, row_tables, col_tables)

    hits = sum(
        ((pert_ref[p] >= first) & (pert_ref[p] < first + STEP)).astype(jnp.int32)
        for p in range(pert_count)
    )

    @pl.when(hits > 0)
    def _():
        for t in range(STEP):
            found = sum((pert_ref[p] == first + t).astype(jnp.int32) for p in range(pert_count))

            @pl.when(found > 0)
            def _():
                total = tiles[t].astype(F32)
                for p in range(pert_count):
                    total = total + jnp.where(pert_ref[p] == first + t, perts[p].astype(F32), 0.0)
                tiles[t] = total.astype(BF16)

    def put(t, both, given, kept, row_first):
        cross = both[:HALF, HALF:], both[HALF:, :HALF]
        given[0, t] = both[:HALF, :HALF]
        given[1, t] = cross[0 if row_first else 1]
        kept[0, t] = cross[1 if row_first else 0]
        kept[1, t] = both[HALF:, HALF:]

    def compute(given, kept, row_first):
        for t in range(STEP):
            i = lax.div(index_ref[first + t], tiles_col)
            rows[t] = jnp.dot(row_tables[i], tiles[t], preferred_element_type=F32).astype(BF16)
        for t in range(STEP):
            j = lax.rem(index_ref[first + t], tiles_col)
            both = jnp.dot(rows[t], col_tables[j], preferred_element_type=F32).astype(BF16)
            put(t, both, given, kept, row_first)

    @pl.when(step < row_steps)
    def _():
        compute(row_given, row_kept, True)
        if with_features:
            for t in range(features.shape[0]):
                table = row_tables[lane_ref[0] * features.shape[0] + t]
                both = jnp.dot(table, features[t], preferred_element_type=F32).astype(BF16)
                put(STEP + t, both, row_given, row_kept, True)

    @pl.when(step >= row_steps)
    def _():
        compute(col_given, col_kept, False)


def pair_tiles(
    starts, counts, index, pert_slot, lane, tile_values, partner, pert_values, features, sizes, token
):
    tiles_row, tiles_col = sizes
    row_steps, col_steps = counts[0] // STEP, counts[1] // STEP
    row_block, col_block = starts[0] // STEP, starts[1] // STEP
    with_features = features is not None
    extra = features.shape[0] // LANES if with_features else 0

    def tile_map(s, *_):
        return (jnp.where(s < row_steps, row_block + s, col_block + s - row_steps), 0, 0)

    shapes = [
        jax.ShapeDtypeStruct((2, count, HALF, HALF), BF16)
        for count in (counts[0] + extra,) * 2 + (counts[1],) * 2
    ]
    if with_features:
        row_out = full(shapes[0].shape)
    else:
        row_out = pl.BlockSpec(
            (2, STEP, HALF, HALF), lambda s, *_: (0, jnp.minimum(s, row_steps - 1), 0, 0)
        )
    col_out = pl.BlockSpec(
        (2, STEP, HALF, HALF), lambda s, *_: (0, jnp.maximum(s - row_steps, 0), 0, 0)
    )
    in_specs = [
        pl.BlockSpec((STEP, TILE, TILE), tile_map),
        full(partner.shape),
        full(pert_values.shape),
    ]
    operands = [tile_values, partner, pert_values]
    if with_features:
        in_specs.append(
            pl.BlockSpec((extra,) + features.shape[1:], lambda s, a, b, lane: (lane[0], 0, 0))
        )
        operands.append(features)
    return pl.pallas_call(
        functools.partial(pair_kernel, starts, counts, with_features),
        out_shape=shapes,
        grid_spec=pltpu.PrefetchScalarGridSpec(
            num_scalar_prefetch=3,
            grid=(row_steps + col_steps,),
            in_specs=in_specs + [ANYWHERE],
            out_specs=[row_out, row_out, col_out, col_out],
            scratch_shapes=[
                pltpu.VMEM((tiles_row, TILE, TILE), BF16),
                pltpu.VMEM((tiles_col, TILE, TILE), BF16),
                pltpu.VMEM((STEP, TILE, TILE), BF16),
            ],
        ),
        compiler_params=PARAMS,
        name="pair_tiles",
    )(index, pert_slot, lane, *operands, token)


def sum_kernel(bounds, tiles_col, index_ref, *rest):
    pieces, sums, total = rest[:-2], rest[-2], rest[-1]
    step = pl.program_id(0)

    @pl.when(step == 0)
    def _():
        total[...] = jnp.zeros_like(total)

    for number, (begin, steps, start, row_first) in enumerate(bounds):
        given, kept = pieces[2 * number], pieces[2 * number + 1]

        @pl.when((step >= begin) & (step < begin + steps))
        def _():
            for t in range(STEP):
                i = lax.div(index_ref[start + (step - begin) * STEP + t], tiles_col)
                cross = given[1, t].astype(F32), kept[0, t].astype(F32)
                given_part, kept_part = cross if row_first else cross[::-1]
                total[0, i] += given[0, t].astype(F32) + given_part
                total[1, i] += kept[1, t].astype(F32) + kept_part

    @pl.when(step == pl.num_programs(0) - 1)
    def _():
        row_side = position()[0]
        for i in range(total.shape[1]):
            given_line = jnp.sum(total[0, i].T, axis=0, keepdims=True)
            kept_line = jnp.sum(total[1, i].T, axis=0, keepdims=True)
            sums[i : i + 1, :HALF] = jnp.where(row_side == 1, given_line, kept_line)
            sums[i : i + 1, HALF:] = jnp.where(row_side == 1, kept_line, given_line)


def sum_rows(pieces, index, sizes):
    tiles_row, tiles_col = sizes
    bounds, specs, operands = [], [], []
    begin = 0
    for piece in pieces:
        steps = piece["count"] // STEP

        def block_map(s, *_, begin=begin, steps=steps):
            return (0, jnp.clip(s - begin, 0, steps - 1), 0, 0)

        specs += [pl.BlockSpec((2, STEP, HALF, HALF), block_map)] * 2
        operands += [piece["given"], piece["kept"]]
        bounds.append((begin, steps, piece["start"], piece["row_first"]))
        begin += steps
    return pl.pallas_call(
        functools.partial(sum_kernel, bounds, tiles_col),
        out_shape=jax.ShapeDtypeStruct((tiles_row, TILE), F32),
        grid_spec=pltpu.PrefetchScalarGridSpec(
            num_scalar_prefetch=1,
            grid=(begin,),
            in_specs=specs,
            out_specs=full((tiles_row, TILE)),
            scratch_shapes=[pltpu.VMEM((2, tiles_row, HALF, HALF), F32)],
        ),
        compiler_params=PARAMS,
        name="sum_rows",
    )(index, *operands)


def line_kernel(spread, _, out):
    line = jnp.sum(spread[...], axis=0, keepdims=True)
    out[...] = jnp.broadcast_to(line, out.shape)


def line_copies(spread, devices, token):
    return pl.pallas_call(
        line_kernel,
        out_shape=jax.ShapeDtypeStruct((devices, TILE), F32),
        in_specs=[pl.BlockSpec(memory_space=pltpu.VMEM), ANYWHERE],
        out_specs=pl.BlockSpec(memory_space=pltpu.VMEM),
        compiler_params=PARAMS,
        name="line_copies",
    )(spread, token)


def forward_kernel(steps, *refs):
    row_kept, row_came, col_kept, col_came = refs[:4]
    row_given, col_given = refs[-2:]
    step = pl.program_id(0)

    def both(kept, came, given):
        given[...] = (kept[0].astype(F32) + came[0].astype(F32)).astype(BF16)

    pl.when(step < steps[0])(lambda: both(row_kept, row_came, row_given))
    pl.when(step < steps[1])(lambda: both(col_kept, col_came, col_given))


def quadrant(which, steps):
    return pl.BlockSpec(
        (1, STEP, HALF, HALF), lambda s, *_: (which, jnp.minimum(s, steps - 1), 0, 0)
    )


def plain(steps):
    return pl.BlockSpec((STEP, HALF, HALF), lambda s, *_: (jnp.minimum(s, steps - 1), 0, 0))


def forward(pair, tokens):
    steps = [piece["count"] // STEP for piece in pair]
    operands = [piece[key] for piece in pair for key in ("kept", "came")]
    return pl.pallas_call(
        functools.partial(forward_kernel, steps),
        out_shape=[jax.ShapeDtypeStruct((piece["count"], HALF, HALF), BF16) for piece in pair],
        grid=(max(steps),),
        in_specs=[quadrant(0, steps[k // 2]) for k in range(4)] + [ANYWHERE] * len(tokens),
        out_specs=[plain(steps[0]), plain(steps[1])],
        compiler_params=PARAMS,
        name="forward",
    )(*operands, *tokens)


def zero_kernel(_, out):
    out[...] = jnp.zeros_like(out)


def zero_buffer(count, token):
    return pl.pallas_call(
        zero_kernel,
        out_shape=jax.ShapeDtypeStruct((count, HALF, HALF), BF16),
        grid=(count // 64,),
        in_specs=[ANYWHERE],
        out_specs=pl.BlockSpec((64, HALF, HALF), lambda s: (s, 0, 0)),
        compiler_params=PARAMS,
        name="zero_buffer",
    )(token)


def store_roots(raw, scale):
    half = raw.shape[0] // 2
    total = raw[:half] + raw[half:]
    roots = 1.0 / jnp.sqrt(1.0 + total / (total.shape[0] * total.shape[1]))
    scale[0] = roots[:, :HALF]
    scale[1] = roots[:, HALF:]


def upright(line):
    return jnp.broadcast_to(line, (HALF, HALF)).T


def finish_kernel(starts, counts, index_ref, place_ref, *refs):
    pieces, raw = (refs[0:3], refs[3:6]), refs[6]
    out, scale, row_scale, col_scale, done, sem = refs[-6:]
    tiles_row = row_scale.shape[0]
    tiles_col = col_scale.shape[0]
    step = pl.program_id(0)

    @pl.when(step == 0)
    def _():
        row_side, row_group, col_side, col_group = position()
        store_roots(raw, scale)
        for i in range(tiles_row):
            row_scale[i] = upright(scale[row_side, pl.ds(row_group * tiles_row + i, 1), :])
        for j in range(tiles_col):
            line = scale[col_side, pl.ds(col_group * tiles_col + j, 1), :]
            col_scale[j] = jnp.broadcast_to(line, (8, HALF))

    for number in range(2):
        kept, came, last = pieces[number]
        base = number * counts[0]

        @pl.when(step < counts[number] // STEP)
        def _():
            for t in range(STEP):
                m = step * STEP + t
                n = starts[number] + m
                i = lax.div(index_ref[n], tiles_col)
                j = lax.rem(index_ref[n], tiles_col)
                total = kept[0, t].astype(F32) + came[0, t].astype(F32) + last[t].astype(F32)
                done[base + m] = (total * row_scale[i] * col_scale[j, 0:1]).astype(BF16)
                pltpu.make_async_copy(done.at[base + m], out.at[place_ref[n]], sem).start()

    @pl.when(step == pl.num_programs(0) - 1)
    def _():
        pltpu.make_async_copy(done, out.at[pl.ds(0, done.shape[0])], sem).wait()


def finish(pair, index, place, raw, buffer, sizes, token):
    tiles_row, tiles_col = sizes
    starts = [piece["start"] for piece in pair]
    counts = [piece["count"] for piece in pair]
    specs, operands = [], []
    for piece in pair:
        steps = piece["count"] // STEP
        specs += [quadrant(1, steps), quadrant(1, steps), plain(steps)]
        operands += [piece["kept"], piece["came"], piece["last"]]
    return pl.pallas_call(
        functools.partial(finish_kernel, starts, counts),
        out_shape=jax.ShapeDtypeStruct(buffer.shape, BF16),
        grid_spec=pltpu.PrefetchScalarGridSpec(
            num_scalar_prefetch=2,
            grid=(max(counts) // STEP,),
            in_specs=specs + [full(raw.shape), ANYWHERE, ANYWHERE],
            out_specs=ANYWHERE,
            scratch_shapes=[
                pltpu.VMEM((2, raw.shape[0] // 2, HALF), F32),
                pltpu.VMEM((tiles_row, HALF, HALF), F32),
                pltpu.VMEM((tiles_col, 8, HALF), F32),
                pltpu.VMEM((sum(counts), HALF, HALF), BF16),
                pltpu.SemaphoreType.DMA,
            ],
        ),
        input_output_aliases={9: 0},
        compiler_params=PARAMS,
        name="finish",
    )(index, place, *operands, raw, buffer, token)


def join_kernel(tiles_row, lane_ref, kept, came, weight, raw, _, out, scale):
    row_side, row_group, _, _ = position()
    part = out.shape[0]
    store_roots(raw, scale)
    for t in range(part):
        merged = [
            (kept[h, t].astype(F32) + came[h, t].astype(F32)).astype(BF16) for h in range(2)
        ]
        joined = jnp.dot(
            jnp.concatenate(merged, axis=1), weight[...], preferred_element_type=F32
        )
        k = row_group * tiles_row + lane_ref[0] * part + t
        column = upright(scale[row_side, pl.ds(k, 1), :])
        out[t] = (joined * jnp.concatenate([column] * 2, axis=1)).astype(BF16)


def join_features(lane, piece, weight, raw, tiles_row, token):
    part = tiles_row // LANES
    block = pl.BlockSpec((2, part, HALF, HALF), lambda s, *_: (0, piece["count"] // part, 0, 0))
    shape = (part, HALF, weight.shape[1])
    return pl.pallas_call(
        functools.partial(join_kernel, tiles_row),
        out_shape=jax.ShapeDtypeStruct(shape, BF16),
        grid_spec=pltpu.PrefetchScalarGridSpec(
            num_scalar_prefetch=1,
            grid=(1,),
            in_specs=[block, block, full(weight.shape), full(raw.shape), ANYWHERE],
            out_specs=full(shape),
            scratch_shapes=[pltpu.VMEM((2, raw.shape[0] // 2, HALF), F32)],
        ),
        compiler_params=PARAMS,
        name="join_features",
    )(lane, piece["kept"], piece["came"], weight, raw, token)


def assemble_kernel(*refs):
    shared, out = refs[:LANES], refs[-1]
    part = shared[0].shape[0]
    lane = lax.rem(lax.axis_index("col"), LANES)
    for shift in range(LANES):
        owner = lax.rem(lane + LANES - shift, LANES)
        out[pl.ds(owner * part, part)] = shared[shift][...]


def assemble(shared, token):
    part = shared[0].shape[0]
    inner = shared[0].shape[1:]
    shape = (LANES * part,) + inner
    return pl.pallas_call(
        assemble_kernel,
        out_shape=jax.ShapeDtypeStruct(shape, BF16),
        grid=(1,),
        in_specs=[full((part,) + inner)] * LANES + [ANYWHERE],
        out_specs=full(shape),
        compiler_params=PARAMS,
        name="assemble",
    )(*shared, token)


def copy_kernel(parts, source, out, sem):
    size = source.shape[0] // parts

    def move(k):
        window = pl.ds(k * size, size)
        return pltpu.make_async_copy(source.at[window], out.at[window], sem.at[k])

    for k in range(parts):
        move(k).start()
    for k in range(parts):
        move(k).wait()


def copied(source):
    parts = 16
    return pl.pallas_call(
        functools.partial(copy_kernel, parts),
        out_shape=jax.ShapeDtypeStruct(source.shape, source.dtype),
        in_specs=[ANYWHERE],
        out_specs=ANYWHERE,
        scratch_shapes=[pltpu.SemaphoreType.DMA((parts,))],
        compiler_params=pltpu.CompilerParams(vmem_limit_bytes=1 << 20),
        name="copied",
    )(source)


def level(features, join_weight, partner, tile_index, tile_values, pert_slot, pert_values, routes):
    row_count = lax.axis_size("row")
    col_count = lax.axis_size("col")
    devices = row_count * col_count
    masks = ("row", row_count // 2), ("col", col_count // 2)
    slot_count = tile_values.shape[0]
    width = features.shape[1]
    tiles_row = features.shape[0] // TILE
    tiles_col = partner.shape[0] // TILE // col_count
    sizes = tiles_row, tiles_col
    capacity = routes.shape[1]
    chunks = len(CHUNKS)
    lane = (lax.axis_index("col") % LANES).reshape(1)
    partner = partner.reshape(-1, HALF)
    feature_tiles = features.reshape(tiles_row, TILE, width)

    starts = [0, ROW_FIRST]
    token = pert_values
    pairs = []
    for chunk in range(chunks):
        counts = CHUNKS[chunk]
        row_given, row_kept, col_given, col_kept = pair_tiles(
            tuple(starts), counts, tile_index, pert_slot, lane, tile_values, partner,
            pert_values, feature_tiles if chunk == 0 else None, sizes, token,
        )
        token = col_kept
        pair = []
        for kind, (given, kept) in enumerate(((row_given, row_kept), (col_given, col_kept))):
            came = flipped(given, *masks[kind])
            pair.append(
                dict(
                    row_first=kind == 0, start=starts[kind], count=counts[kind],
                    given=given, kept=kept, came=came,
                )
            )
            starts[kind] += counts[kind]
        pairs.append(pair)

    own = sum_rows([piece for pair in pairs for piece in pair], tile_index, sizes)
    spread = lax.all_to_all(own, "col", split_axis=0, concat_axis=0, tiled=True)

    targets = routes[:, 0]
    order = jnp.arange(slot_count, dtype=jnp.int32)
    same = (targets[:, None] == targets[None, :]) & (order[None, :] < order[:, None])
    place = targets * capacity + jnp.sum(same.astype(jnp.int32), axis=1)

    buffer = zero_buffer(devices * capacity, own)
    token = buffer
    for chunk, pair in enumerate(pairs):
        given = forward(pair, [token])
        token = given[0]
        for kind in range(2):
            pair[kind]["last"] = flipped(given[kind], *masks[1 - kind])
        if chunk == 0:
            token = line_copies(spread, devices, token)
            raw = lax.all_to_all(token, ("row", "col"), split_axis=0, concat_axis=0, tiled=True)

    def finished(chunk, buffer, token):
        return finish(pairs[chunk], tile_index, place, raw, buffer, sizes, token)

    buffer = finished(0, buffer, token)
    joined = join_features(lane, pairs[0][0], join_weight, raw, tiles_row, buffer)
    buffer = finished(1, buffer, joined)
    shared = [joined]
    for shift in range(1, LANES):
        ring = [
            (source, source // LANES * LANES + (source + shift) % LANES)
            for source in range(col_count)
        ]
        shared.append(lax.ppermute(joined, "col", ring))
    assembled = assemble(shared, buffer)
    buffer = finished(2, buffer, assembled)
    coarse_features = assembled.reshape(tiles_row * HALF, width)
    arrived = lax.all_to_all(buffer, ("row", "col"), split_axis=0, concat_axis=0, tiled=True)
    return (coarse_features, copied(arrived))


def solution(mesh):
    both = P(("row", "col"))
    placed = (
        P("row", None),
        P(),
        P(),
        both,
        P(("row", "col"), None, None),
        both,
        P(("row", "col"), None, None),
        P(("row", "col"), None),
    )
    return jax.shard_map(
        level,
        mesh=mesh,
        in_specs=placed,
        out_specs=(P("row", None), P(("row", "col"), None, None)),
        check_vma=False,
    )
```

```python
import functools

import jax
import jax.numpy as jnp
from jax import lax
from jax.experimental import pallas as pl
from jax.experimental.pallas import tpu as pltpu
from jax.sharding import PartitionSpec as P


TILE = 256
HALF = 128
STEP = 8
LANES = 4
ROW_FIRST = 48
CHUNKS = (8, 16), (24, 24), (16, 16)
SPLITS = 1, 1, 2
BF16 = jnp.bfloat16
F32 = jnp.float32
PARAMS = pltpu.CompilerParams(vmem_limit_bytes=66_500_000)
ANYWHERE = pl.BlockSpec(memory_space=pl.ANY)


def flipped(value, axis, mask):
    pairs = [(source, source ^ mask) for source in range(lax.axis_size(axis))]
    return lax.ppermute(value, axis, pairs)


def full(shape):
    return pl.BlockSpec(shape, lambda *_: (0,) * len(shape))


def iota(shape, axis):
    return lax.broadcasted_iota(jnp.int32, shape, axis)


def position():
    row_half = lax.axis_size("row") // 2
    col_half = lax.axis_size("col") // 2
    row_index = lax.axis_index("row")
    col_index = lax.axis_index("col")
    return (
        lax.div(row_index, row_half),
        lax.rem(row_index, row_half),
        lax.div(col_index, col_half),
        lax.rem(col_index, col_half),
    )


def build_tables(partner_ref, row_tables, col_tables):
    row_side, row_group, col_side, col_group = position()
    tiles_row = row_tables.shape[0]
    tiles_col = col_tables.shape[0]
    coarse_nodes = partner_ref.shape[0] * HALF // 2
    rotated = (iota((1, TILE), 1) + HALF) & (TILE - 1)
    level = iota((TILE, TILE), 0).astype(F32).astype(BF16)

    def vector(start, shift):
        first = partner_ref[pl.ds(start, 1), :]
        second = partner_ref[pl.ds(start + 1, 1), :]
        return jnp.concatenate([first, second], axis=1) - shift

    def table(values):
        line = values.astype(F32).astype(BF16)
        same = jnp.broadcast_to(line, (TILE, TILE)) == level
        return jnp.where(same, jnp.ones((), BF16), jnp.zeros((), BF16))

    for i in range(tiles_row):
        k = row_group * tiles_row + i
        slots = vector(coarse_nodes // HALF + 2 * k, k * TILE)
        row_tables[i] = table(jnp.where(row_side == 1, slots, rotated))
    for j in range(tiles_col):
        k = col_group * tiles_col + j
        nodes = vector(2 * k, coarse_nodes + k * TILE)
        col_tables[j] = table(jnp.where(col_side == 1, nodes, rotated))


def pair_kernel(
    starts, counts, with_features, index_ref, pert_ref, lane_ref, tiles, partner_ref, perts, *rest
):
    if with_features:
        features, rest = rest[0], rest[1:]
    _, row_given, row_kept, col_given, col_kept, row_tables, col_tables, rows = rest
    tiles_col = col_tables.shape[0]
    step = pl.program_id(0)
    row_steps = counts[0] // STEP
    pert_count = pert_ref.shape[0]
    first = jnp.where(
        step < row_steps, starts[0] + step * STEP, starts[1] + (step - row_steps) * STEP
    )

    @pl.when(step == 0)
    def _():
        build_tables(partner_ref, row_tables, col_tables)

    hits = sum(
        ((pert_ref[p] >= first) & (pert_ref[p] < first + STEP)).astype(jnp.int32)
        for p in range(pert_count)
    )

    @pl.when(hits > 0)
    def _():
        for t in range(STEP):
            found = sum((pert_ref[p] == first + t).astype(jnp.int32) for p in range(pert_count))

            @pl.when(found > 0)
            def _():
                total = tiles[t].astype(F32)
                for p in range(pert_count):
                    total = total + jnp.where(pert_ref[p] == first + t, perts[p].astype(F32), 0.0)
                tiles[t] = total.astype(BF16)

    def put(t, both, given, kept, row_first):
        cross = both[:HALF, HALF:], both[HALF:, :HALF]
        given[0, t] = both[:HALF, :HALF]
        given[1, t] = cross[0 if row_first else 1]
        kept[0, t] = cross[1 if row_first else 0]
        kept[1, t] = both[HALF:, HALF:]

    def compute(given, kept, row_first):
        for t in range(STEP):
            i = lax.div(index_ref[first + t], tiles_col)
            rows[t] = jnp.dot(row_tables[i], tiles[t], preferred_element_type=F32).astype(BF16)
        for t in range(STEP):
            j = lax.rem(index_ref[first + t], tiles_col)
            both = jnp.dot(rows[t], col_tables[j], preferred_element_type=F32).astype(BF16)
            put(t, both, given, kept, row_first)

    @pl.when(step < row_steps)
    def _():
        compute(row_given, row_kept, True)
        if with_features:
            for t in range(features.shape[0]):
                table = row_tables[lane_ref[0] * features.shape[0] + t]
                both = jnp.dot(table, features[t], preferred_element_type=F32).astype(BF16)
                put(STEP + t, both, row_given, row_kept, True)

    @pl.when(step >= row_steps)
    def _():
        compute(col_given, col_kept, False)


def pair_tiles(
    starts, counts, index, pert_slot, lane, tile_values, partner, pert_values, features, sizes, token
):
    tiles_row, tiles_col = sizes
    row_steps, col_steps = counts[0] // STEP, counts[1] // STEP
    row_block, col_block = starts[0] // STEP, starts[1] // STEP
    with_features = features is not None
    extra = features.shape[0] // LANES if with_features else 0

    def tile_map(s, *_):
        return (jnp.where(s < row_steps, row_block + s, col_block + s - row_steps), 0, 0)

    shapes = [
        jax.ShapeDtypeStruct((2, count, HALF, HALF), BF16)
        for count in (counts[0] + extra,) * 2 + (counts[1],) * 2
    ]
    if with_features:
        row_out = full(shapes[0].shape)
    else:
        row_out = pl.BlockSpec(
            (2, STEP, HALF, HALF), lambda s, *_: (0, jnp.minimum(s, row_steps - 1), 0, 0)
        )
    col_out = pl.BlockSpec(
        (2, STEP, HALF, HALF), lambda s, *_: (0, jnp.maximum(s - row_steps, 0), 0, 0)
    )
    in_specs = [
        pl.BlockSpec((STEP, TILE, TILE), tile_map),
        full(partner.shape),
        full(pert_values.shape),
    ]
    operands = [tile_values, partner, pert_values]
    if with_features:
        in_specs.append(
            pl.BlockSpec((extra,) + features.shape[1:], lambda s, a, b, lane: (lane[0], 0, 0))
        )
        operands.append(features)
    return pl.pallas_call(
        functools.partial(pair_kernel, starts, counts, with_features),
        out_shape=shapes,
        grid_spec=pltpu.PrefetchScalarGridSpec(
            num_scalar_prefetch=3,
            grid=(row_steps + col_steps,),
            in_specs=in_specs + [ANYWHERE],
            out_specs=[row_out, row_out, col_out, col_out],
            scratch_shapes=[
                pltpu.VMEM((tiles_row, TILE, TILE), BF16),
                pltpu.VMEM((tiles_col, TILE, TILE), BF16),
                pltpu.VMEM((STEP, TILE, TILE), BF16),
            ],
        ),
        compiler_params=PARAMS,
        name="pair_tiles",
    )(index, pert_slot, lane, *operands, token)


def sum_kernel(bounds, tiles_col, index_ref, *rest):
    pieces, sums, total = rest[:-2], rest[-2], rest[-1]
    step = pl.program_id(0)

    @pl.when(step == 0)
    def _():
        total[...] = jnp.zeros_like(total)

    for number, (begin, steps, start, row_first) in enumerate(bounds):
        given, kept = pieces[2 * number], pieces[2 * number + 1]

        @pl.when((step >= begin) & (step < begin + steps))
        def _():
            for t in range(STEP):
                i = lax.div(index_ref[start + (step - begin) * STEP + t], tiles_col)
                cross = given[1, t].astype(F32), kept[0, t].astype(F32)
                given_part, kept_part = cross if row_first else cross[::-1]
                total[0, i] += given[0, t].astype(F32) + given_part
                total[1, i] += kept[1, t].astype(F32) + kept_part

    @pl.when(step == pl.num_programs(0) - 1)
    def _():
        row_side = position()[0]
        for i in range(total.shape[1]):
            given_line = jnp.sum(total[0, i].T, axis=0, keepdims=True)
            kept_line = jnp.sum(total[1, i].T, axis=0, keepdims=True)
            sums[i : i + 1, :HALF] = jnp.where(row_side == 1, given_line, kept_line)
            sums[i : i + 1, HALF:] = jnp.where(row_side == 1, kept_line, given_line)


def sum_rows(pieces, index, sizes):
    tiles_row, tiles_col = sizes
    bounds, specs, operands = [], [], []
    begin = 0
    for piece in pieces:
        steps = piece["count"] // STEP

        def block_map(s, *_, begin=begin, steps=steps):
            return (0, jnp.clip(s - begin, 0, steps - 1), 0, 0)

        specs += [pl.BlockSpec((2, STEP, HALF, HALF), block_map)] * 2
        operands += [piece["given"], piece["kept"]]
        bounds.append((begin, steps, piece["start"], piece["row_first"]))
        begin += steps
    return pl.pallas_call(
        functools.partial(sum_kernel, bounds, tiles_col),
        out_shape=jax.ShapeDtypeStruct((tiles_row, TILE), F32),
        grid_spec=pltpu.PrefetchScalarGridSpec(
            num_scalar_prefetch=1,
            grid=(begin,),
            in_specs=specs,
            out_specs=full((tiles_row, TILE)),
            scratch_shapes=[pltpu.VMEM((2, tiles_row, HALF, HALF), F32)],
        ),
        compiler_params=PARAMS,
        name="sum_rows",
    )(index, *operands)


def line_kernel(spread, _, out):
    line = jnp.sum(spread[...], axis=0, keepdims=True)
    out[...] = jnp.broadcast_to(line, out.shape)


def line_copies(spread, devices, token):
    return pl.pallas_call(
        line_kernel,
        out_shape=jax.ShapeDtypeStruct((devices, TILE), F32),
        in_specs=[pl.BlockSpec(memory_space=pltpu.VMEM), ANYWHERE],
        out_specs=pl.BlockSpec(memory_space=pltpu.VMEM),
        compiler_params=PARAMS,
        name="line_copies",
    )(spread, token)


def forward_kernel(steps, parts, *refs):
    row_kept, row_came, col_kept, col_came = refs[:4]
    row_given, col_given = refs[-2 * parts : -parts], refs[-parts:]
    step = pl.program_id(0)
    size = HALF // parts

    def both(kept, came, given):
        total = (kept[0].astype(F32) + came[0].astype(F32)).astype(BF16)
        for h in range(parts):
            given[h][...] = total[:, h * size : (h + 1) * size]

    pl.when(step < steps[0])(lambda: both(row_kept, row_came, row_given))
    pl.when(step < steps[1])(lambda: both(col_kept, col_came, col_given))


def quadrant(which, steps, size=HALF, h=0):
    return pl.BlockSpec(
        (1, STEP, size, HALF), lambda s, *_: (which, jnp.minimum(s, steps - 1), h, 0)
    )


def plain(steps, size=HALF, h=0):
    return pl.BlockSpec((STEP, size, HALF), lambda s, *_: (jnp.minimum(s, steps - 1), h, 0))


def forward(pair, parts, tokens):
    steps = [piece["count"] // STEP for piece in pair]
    operands = [piece[key] for piece in pair for key in ("kept", "came")]
    size = HALF // parts
    return pl.pallas_call(
        functools.partial(forward_kernel, steps, parts),
        out_shape=[
            jax.ShapeDtypeStruct((piece["count"], size, HALF), BF16)
            for piece in pair
            for _ in range(parts)
        ],
        grid=(max(steps),),
        in_specs=[quadrant(0, steps[k // 2]) for k in range(4)] + [ANYWHERE] * len(tokens),
        out_specs=[plain(steps[k], size) for k in range(2) for _ in range(parts)],
        compiler_params=PARAMS,
        name="forward",
    )(*operands, *tokens)


def zero_kernel(_, out):
    out[...] = jnp.zeros_like(out)


def zero_buffer(count, token):
    return pl.pallas_call(
        zero_kernel,
        out_shape=jax.ShapeDtypeStruct((count, HALF, HALF), BF16),
        grid=(count // 64,),
        in_specs=[ANYWHERE],
        out_specs=pl.BlockSpec((64, HALF, HALF), lambda s: (s, 0, 0)),
        compiler_params=PARAMS,
        name="zero_buffer",
    )(token)


def store_roots(raw, scale):
    half = raw.shape[0] // 2
    total = raw[:half] + raw[half:]
    roots = 1.0 / jnp.sqrt(1.0 + total / (total.shape[0] * total.shape[1]))
    scale[0] = roots[:, :HALF]
    scale[1] = roots[:, HALF:]


def upright(line):
    return jnp.broadcast_to(line, (HALF, HALF)).T


def finish_kernel(starts, counts, h, index_ref, place_ref, *refs):
    total_pieces = len(starts)
    raw = refs[3 * total_pieces]
    out, scale, row_scale, col_scale, done, sem = refs[-6:]
    tiles_row, size, _ = row_scale.shape
    tiles_col = col_scale.shape[0]
    step = pl.program_id(0)

    @pl.when(step == 0)
    def _():
        row_side, row_group, col_side, col_group = position()
        store_roots(raw, scale)
        for i in range(tiles_row):
            column = upright(scale[row_side, pl.ds(row_group * tiles_row + i, 1), :])
            row_scale[i] = column[h * size : (h + 1) * size]
        for j in range(tiles_col):
            line = scale[col_side, pl.ds(col_group * tiles_col + j, 1), :]
            col_scale[j] = jnp.broadcast_to(line, (8, HALF))

    base = 0
    for number in range(total_pieces):
        kept, came, last = refs[3 * number : 3 * number + 3]

        @pl.when(step < counts[number] // STEP)
        def _(kept=kept, came=came, last=last, base=base, start=starts[number]):
            for t in range(STEP):
                m = step * STEP + t
                i = lax.div(index_ref[start + m], tiles_col)
                j = lax.rem(index_ref[start + m], tiles_col)
                total = kept[0, t].astype(F32) + came[0, t].astype(F32) + last[t].astype(F32)
                done[base + m] = (total * row_scale[i] * col_scale[j, 0:1]).astype(BF16)
                target = out.at[place_ref[start + m], pl.ds(h * size, size)]
                pltpu.make_async_copy(done.at[base + m], target, sem).start()

        base += counts[number]

    @pl.when(step == pl.num_programs(0) - 1)
    def _():
        sent = out.at[pl.ds(0, done.shape[0]), pl.ds(0, size)]
        pltpu.make_async_copy(done, sent, sem).wait()


def finish(pieces, h, index, place, raw, buffer, sizes, token):
    tiles_row, tiles_col = sizes
    size = HALF // len(pieces[0]["last"])
    starts = [piece["start"] for piece in pieces]
    counts = [piece["count"] for piece in pieces]
    specs, operands = [], []
    for piece in pieces:
        steps = piece["count"] // STEP
        specs += [quadrant(1, steps, size, h)] * 2 + [plain(steps, size)]
        operands += [piece["kept"], piece["came"], piece["last"][h]]
    return pl.pallas_call(
        functools.partial(finish_kernel, starts, counts, h),
        out_shape=jax.ShapeDtypeStruct(buffer.shape, BF16),
        grid_spec=pltpu.PrefetchScalarGridSpec(
            num_scalar_prefetch=2,
            grid=(max(counts) // STEP,),
            in_specs=specs + [full(raw.shape), ANYWHERE, ANYWHERE],
            out_specs=ANYWHERE,
            scratch_shapes=[
                pltpu.VMEM((2, raw.shape[0] // 2, HALF), F32),
                pltpu.VMEM((tiles_row, size, HALF), F32),
                pltpu.VMEM((tiles_col, 8, HALF), F32),
                pltpu.VMEM((sum(counts), size, HALF), BF16),
                pltpu.SemaphoreType.DMA,
            ],
        ),
        input_output_aliases={3 + len(operands): 0},
        compiler_params=PARAMS,
        name="finish",
    )(index, place, *operands, raw, buffer, token)


def join_kernel(tiles_row, lane_ref, kept, came, weight, raw, _, out, scale):
    row_side, row_group, _, _ = position()
    part = out.shape[0]
    store_roots(raw, scale)
    for t in range(part):
        merged = [
            (kept[h, t].astype(F32) + came[h, t].astype(F32)).astype(BF16) for h in range(2)
        ]
        joined = jnp.dot(
            jnp.concatenate(merged, axis=1), weight[...], preferred_element_type=F32
        )
        k = row_group * tiles_row + lane_ref[0] * part + t
        column = upright(scale[row_side, pl.ds(k, 1), :])
        out[t] = (joined * jnp.concatenate([column] * 2, axis=1)).astype(BF16)


def join_features(lane, piece, weight, raw, tiles_row, token):
    part = tiles_row // LANES
    block = pl.BlockSpec((2, part, HALF, HALF), lambda s, *_: (0, piece["count"] // part, 0, 0))
    shape = (part, HALF, weight.shape[1])
    return pl.pallas_call(
        functools.partial(join_kernel, tiles_row),
        out_shape=jax.ShapeDtypeStruct(shape, BF16),
        grid_spec=pltpu.PrefetchScalarGridSpec(
            num_scalar_prefetch=1,
            grid=(1,),
            in_specs=[block, block, full(weight.shape), full(raw.shape), ANYWHERE],
            out_specs=full(shape),
            scratch_shapes=[pltpu.VMEM((2, raw.shape[0] // 2, HALF), F32)],
        ),
        compiler_params=PARAMS,
        name="join_features",
    )(lane, piece["kept"], piece["came"], weight, raw, token)


def copy_kernel(pieces, *refs):
    source, shared = refs[0], refs[1 : 1 + LANES]
    out, features, held, sem, in_sem, out_sem = refs[1 + LANES :]
    size = source.shape[0] // pieces
    part = held.shape[1]
    lane = lax.rem(lax.axis_index("col"), LANES)

    def move(k):
        window = pl.ds(k * size, size)
        return pltpu.make_async_copy(source.at[window], out.at[window], sem.at[k])

    def read(k):
        return pltpu.make_async_copy(shared[k], held.at[k], in_sem.at[k])

    def write(k):
        owner = lax.rem(lane + LANES - k, LANES)
        target = features.at[pl.ds(owner * part, part)]
        return pltpu.make_async_copy(held.at[k], target, out_sem.at[k])

    for k in range(LANES):
        read(k).start()
    for k in range(pieces):
        move(k).start()
    for k in range(LANES):
        read(k).wait()
        write(k).start()
    for k in range(pieces):
        move(k).wait()
    for k in range(LANES):
        write(k).wait()


def copied(source, shared):
    pieces = 16
    part = shared[0].shape
    return pl.pallas_call(
        functools.partial(copy_kernel, pieces),
        out_shape=[
            jax.ShapeDtypeStruct(source.shape, source.dtype),
            jax.ShapeDtypeStruct((LANES * part[0],) + part[1:], BF16),
        ],
        in_specs=[ANYWHERE] * (1 + LANES),
        out_specs=[ANYWHERE, ANYWHERE],
        scratch_shapes=[
            pltpu.VMEM((LANES,) + part, BF16),
            pltpu.SemaphoreType.DMA((pieces,)),
            pltpu.SemaphoreType.DMA((LANES,)),
            pltpu.SemaphoreType.DMA((LANES,)),
        ],
        compiler_params=pltpu.CompilerParams(vmem_limit_bytes=2 << 20),
        name="copied",
    )(source, *shared)


def level(features, join_weight, partner, tile_index, tile_values, pert_slot, pert_values, routes):
    row_count = lax.axis_size("row")
    col_count = lax.axis_size("col")
    devices = row_count * col_count
    masks = ("row", row_count // 2), ("col", col_count // 2)
    slot_count = tile_values.shape[0]
    width = features.shape[1]
    tiles_row = features.shape[0] // TILE
    tiles_col = partner.shape[0] // TILE // col_count
    sizes = tiles_row, tiles_col
    capacity = routes.shape[1]
    chunks = len(CHUNKS)
    lane = (lax.axis_index("col") % LANES).reshape(1)
    partner = partner.reshape(-1, HALF)
    feature_tiles = features.reshape(tiles_row, TILE, width)

    starts = [0, ROW_FIRST]
    token = pert_values
    pairs = []
    for chunk in range(chunks):
        counts = CHUNKS[chunk]
        row_given, row_kept, col_given, col_kept = pair_tiles(
            tuple(starts), counts, tile_index, pert_slot, lane, tile_values, partner,
            pert_values, feature_tiles if chunk == 0 else None, sizes, token,
        )
        token = col_kept
        pair = []
        for kind, (given, kept) in enumerate(((row_given, row_kept), (col_given, col_kept))):
            came = flipped(given, *masks[kind])
            pair.append(
                dict(
                    row_first=kind == 0, start=starts[kind], count=counts[kind],
                    given=given, kept=kept, came=came,
                )
            )
            starts[kind] += counts[kind]
        pairs.append(pair)

    own = sum_rows([piece for pair in pairs for piece in pair], tile_index, sizes)
    spread = lax.all_to_all(own, "col", split_axis=0, concat_axis=0, tiled=True)

    targets = routes[:, 0]
    order = jnp.arange(slot_count, dtype=jnp.int32)
    same = (targets[:, None] == targets[None, :]) & (order[None, :] < order[:, None])
    place = targets * capacity + jnp.sum(same.astype(jnp.int32), axis=1)

    buffer = zero_buffer(devices * capacity, own)
    token = buffer
    for chunk, pair in enumerate(pairs):
        splits = SPLITS[chunk]
        given = forward(pair, splits, [token])
        token = given[0]
        for kind in range(2):
            pair[kind]["last"] = []
            for h in range(splits):
                last = flipped(given[kind * splits + h], *masks[1 - kind])
                pair[kind]["last"].append(last)
        if chunk == 0:
            token = line_copies(spread, devices, token)
            raw = lax.all_to_all(token, ("row", "col"), split_axis=0, concat_axis=0, tiled=True)

    joined = join_features(lane, pairs[0][0], join_weight, raw, tiles_row, token)
    shared = [joined]
    for shift in range(1, LANES):
        ring = [
            (source, source // LANES * LANES + (source + shift) % LANES)
            for source in range(col_count)
        ]
        shared.append(lax.ppermute(joined, "col", ring))
    for chunk, pair in enumerate(pairs):
        for h in range(SPLITS[chunk]):
            buffer = finish(pair, h, tile_index, place, raw, buffer, sizes, joined)
    arrived = lax.all_to_all(buffer, ("row", "col"), split_axis=0, concat_axis=0, tiled=True)
    result, coarse_features = copied(arrived, shared)
    return (coarse_features.reshape(tiles_row * HALF, width), result)


def solution(mesh):
    both = P(("row", "col"))
    placed = (
        P("row", None),
        P(),
        P(),
        both,
        P(("row", "col"), None, None),
        both,
        P(("row", "col"), None, None),
        P(("row", "col"), None),
    )
    return jax.shard_map(
        level,
        mesh=mesh,
        in_specs=placed,
        out_specs=(P("row", None), P(("row", "col"), None, None)),
        check_vma=False,
    )
```

```python
import functools

import jax
import jax.numpy as jnp
from jax import lax
from jax.experimental import pallas as pl
from jax.experimental.pallas import tpu as pltpu
from jax.sharding import PartitionSpec as P


TILE = 256
HALF = 128
STEP = 8
LANES = 4
ROW_FIRST = 48
CHUNKS = (8, 8), (8, 16), (16, 16), (16, 16)
SPLITS = 1, 1, 1, 1
BF16 = jnp.bfloat16
F32 = jnp.float32
PARAMS = pltpu.CompilerParams(vmem_limit_bytes=66_500_000)
ANYWHERE = pl.BlockSpec(memory_space=pl.ANY)


def flipped(value, axis, mask):
    pairs = [(source, source ^ mask) for source in range(lax.axis_size(axis))]
    return lax.ppermute(value, axis, pairs)


def full(shape):
    return pl.BlockSpec(shape, lambda *_: (0,) * len(shape))


def iota(shape, axis):
    return lax.broadcasted_iota(jnp.int32, shape, axis)


def position():
    row_half = lax.axis_size("row") // 2
    col_half = lax.axis_size("col") // 2
    row_index = lax.axis_index("row")
    col_index = lax.axis_index("col")
    return (
        lax.div(row_index, row_half),
        lax.rem(row_index, row_half),
        lax.div(col_index, col_half),
        lax.rem(col_index, col_half),
    )


def build_tables(partner_ref, row_tables, col_tables):
    row_side, row_group, col_side, col_group = position()
    tiles_row = row_tables.shape[0]
    tiles_col = col_tables.shape[0]
    coarse_nodes = partner_ref.shape[0] * HALF // 2
    rotated = (iota((1, TILE), 1) + HALF) & (TILE - 1)
    level = iota((TILE, TILE), 0).astype(F32).astype(BF16)

    def vector(start, shift):
        first = partner_ref[pl.ds(start, 1), :]
        second = partner_ref[pl.ds(start + 1, 1), :]
        return jnp.concatenate([first, second], axis=1) - shift

    def table(values):
        line = values.astype(F32).astype(BF16)
        same = jnp.broadcast_to(line, (TILE, TILE)) == level
        return jnp.where(same, jnp.ones((), BF16), jnp.zeros((), BF16))

    for i in range(tiles_row):
        k = row_group * tiles_row + i
        slots = vector(coarse_nodes // HALF + 2 * k, k * TILE)
        row_tables[i] = table(jnp.where(row_side == 1, slots, rotated))
    for j in range(tiles_col):
        k = col_group * tiles_col + j
        nodes = vector(2 * k, coarse_nodes + k * TILE)
        col_tables[j] = table(jnp.where(col_side == 1, nodes, rotated))


def pair_kernel(
    starts, counts, with_features, index_ref, pert_ref, lane_ref, tiles, partner_ref, perts, *rest
):
    if with_features:
        features, rest = rest[0], rest[1:]
    _, row_given, row_kept, col_given, col_kept, row_tables, col_tables, rows = rest
    tiles_col = col_tables.shape[0]
    step = pl.program_id(0)
    row_steps = counts[0] // STEP
    pert_count = pert_ref.shape[0]
    first = jnp.where(
        step < row_steps, starts[0] + step * STEP, starts[1] + (step - row_steps) * STEP
    )

    @pl.when(step == 0)
    def _():
        build_tables(partner_ref, row_tables, col_tables)

    hits = sum(
        ((pert_ref[p] >= first) & (pert_ref[p] < first + STEP)).astype(jnp.int32)
        for p in range(pert_count)
    )

    @pl.when(hits > 0)
    def _():
        for t in range(STEP):
            found = sum((pert_ref[p] == first + t).astype(jnp.int32) for p in range(pert_count))

            @pl.when(found > 0)
            def _():
                total = tiles[t].astype(F32)
                for p in range(pert_count):
                    total = total + jnp.where(pert_ref[p] == first + t, perts[p].astype(F32), 0.0)
                tiles[t] = total.astype(BF16)

    def put(t, both, given, kept, row_first):
        cross = both[:HALF, HALF:], both[HALF:, :HALF]
        given[0, t] = both[:HALF, :HALF]
        given[1, t] = cross[0 if row_first else 1]
        kept[0, t] = cross[1 if row_first else 0]
        kept[1, t] = both[HALF:, HALF:]

    def compute(given, kept, row_first):
        for t in range(STEP):
            i = lax.div(index_ref[first + t], tiles_col)
            rows[t] = jnp.dot(row_tables[i], tiles[t], preferred_element_type=F32).astype(BF16)
        for t in range(STEP):
            j = lax.rem(index_ref[first + t], tiles_col)
            both = jnp.dot(rows[t], col_tables[j], preferred_element_type=F32).astype(BF16)
            put(t, both, given, kept, row_first)

    @pl.when(step < row_steps)
    def _():
        compute(row_given, row_kept, True)
        if with_features:
            for t in range(features.shape[0]):
                table = row_tables[lane_ref[0] * features.shape[0] + t]
                both = jnp.dot(table, features[t], preferred_element_type=F32).astype(BF16)
                put(STEP + t, both, row_given, row_kept, True)

    @pl.when(step >= row_steps)
    def _():
        compute(col_given, col_kept, False)


def pair_tiles(
    starts, counts, index, pert_slot, lane, tile_values, partner, pert_values, features, sizes, token
):
    tiles_row, tiles_col = sizes
    row_steps, col_steps = counts[0] // STEP, counts[1] // STEP
    row_block, col_block = starts[0] // STEP, starts[1] // STEP
    with_features = features is not None
    extra = features.shape[0] // LANES if with_features else 0

    def tile_map(s, *_):
        return (jnp.where(s < row_steps, row_block + s, col_block + s - row_steps), 0, 0)

    shapes = [
        jax.ShapeDtypeStruct((2, count, HALF, HALF), BF16)
        for count in (counts[0] + extra,) * 2 + (counts[1],) * 2
    ]
    if with_features:
        row_out = full(shapes[0].shape)
    else:
        row_out = pl.BlockSpec(
            (2, STEP, HALF, HALF), lambda s, *_: (0, jnp.minimum(s, row_steps - 1), 0, 0)
        )
    col_out = pl.BlockSpec(
        (2, STEP, HALF, HALF), lambda s, *_: (0, jnp.maximum(s - row_steps, 0), 0, 0)
    )
    in_specs = [
        pl.BlockSpec((STEP, TILE, TILE), tile_map),
        full(partner.shape),
        full(pert_values.shape),
    ]
    operands = [tile_values, partner, pert_values]
    if with_features:
        in_specs.append(
            pl.BlockSpec((extra,) + features.shape[1:], lambda s, a, b, lane: (lane[0], 0, 0))
        )
        operands.append(features)
    return pl.pallas_call(
        functools.partial(pair_kernel, starts, counts, with_features),
        out_shape=shapes,
        grid_spec=pltpu.PrefetchScalarGridSpec(
            num_scalar_prefetch=3,
            grid=(row_steps + col_steps,),
            in_specs=in_specs + [ANYWHERE],
            out_specs=[row_out, row_out, col_out, col_out],
            scratch_shapes=[
                pltpu.VMEM((tiles_row, TILE, TILE), BF16),
                pltpu.VMEM((tiles_col, TILE, TILE), BF16),
                pltpu.VMEM((STEP, TILE, TILE), BF16),
            ],
        ),
        compiler_params=PARAMS,
        name="pair_tiles",
    )(index, pert_slot, lane, *operands, token)


def sum_kernel(bounds, tiles_col, index_ref, *rest):
    pieces, sums, total = rest[:-2], rest[-2], rest[-1]
    step = pl.program_id(0)

    @pl.when(step == 0)
    def _():
        total[...] = jnp.zeros_like(total)

    for number, (begin, steps, start, row_first) in enumerate(bounds):
        given, kept = pieces[2 * number], pieces[2 * number + 1]

        @pl.when((step >= begin) & (step < begin + steps))
        def _():
            for t in range(STEP):
                i = lax.div(index_ref[start + (step - begin) * STEP + t], tiles_col)
                cross = given[1, t].astype(F32), kept[0, t].astype(F32)
                given_part, kept_part = cross if row_first else cross[::-1]
                total[0, i] += given[0, t].astype(F32) + given_part
                total[1, i] += kept[1, t].astype(F32) + kept_part

    @pl.when(step == pl.num_programs(0) - 1)
    def _():
        row_side = position()[0]
        for i in range(total.shape[1]):
            given_line = jnp.sum(total[0, i].T, axis=0, keepdims=True)
            kept_line = jnp.sum(total[1, i].T, axis=0, keepdims=True)
            sums[i : i + 1, :HALF] = jnp.where(row_side == 1, given_line, kept_line)
            sums[i : i + 1, HALF:] = jnp.where(row_side == 1, kept_line, given_line)


def sum_rows(pieces, index, sizes):
    tiles_row, tiles_col = sizes
    bounds, specs, operands = [], [], []
    begin = 0
    for piece in pieces:
        steps = piece["count"] // STEP

        def block_map(s, *_, begin=begin, steps=steps):
            return (0, jnp.clip(s - begin, 0, steps - 1), 0, 0)

        specs += [pl.BlockSpec((2, STEP, HALF, HALF), block_map)] * 2
        operands += [piece["given"], piece["kept"]]
        bounds.append((begin, steps, piece["start"], piece["row_first"]))
        begin += steps
    return pl.pallas_call(
        functools.partial(sum_kernel, bounds, tiles_col),
        out_shape=jax.ShapeDtypeStruct((tiles_row, TILE), F32),
        grid_spec=pltpu.PrefetchScalarGridSpec(
            num_scalar_prefetch=1,
            grid=(begin,),
            in_specs=specs,
            out_specs=full((tiles_row, TILE)),
            scratch_shapes=[pltpu.VMEM((2, tiles_row, HALF, HALF), F32)],
        ),
        compiler_params=PARAMS,
        name="sum_rows",
    )(index, *operands)


def line_kernel(spread, _, out):
    line = jnp.sum(spread[...], axis=0, keepdims=True)
    out[...] = jnp.broadcast_to(line, out.shape)


def line_copies(spread, devices, token):
    return pl.pallas_call(
        line_kernel,
        out_shape=jax.ShapeDtypeStruct((devices, TILE), F32),
        in_specs=[pl.BlockSpec(memory_space=pltpu.VMEM), ANYWHERE],
        out_specs=pl.BlockSpec(memory_space=pltpu.VMEM),
        compiler_params=PARAMS,
        name="line_copies",
    )(spread, token)


def forward_kernel(steps, parts, *refs):
    row_kept, row_came, col_kept, col_came = refs[:4]
    row_given, col_given = refs[-2 * parts : -parts], refs[-parts:]
    step = pl.program_id(0)
    size = HALF // parts

    def both(kept, came, given):
        total = (kept[0].astype(F32) + came[0].astype(F32)).astype(BF16)
        for h in range(parts):
            given[h][...] = total[:, h * size : (h + 1) * size]

    pl.when(step < steps[0])(lambda: both(row_kept, row_came, row_given))
    pl.when(step < steps[1])(lambda: both(col_kept, col_came, col_given))


def quadrant(which, steps, size=HALF, h=0):
    return pl.BlockSpec(
        (1, STEP, size, HALF), lambda s, *_: (which, jnp.minimum(s, steps - 1), h, 0)
    )


def plain(steps, size=HALF, h=0):
    return pl.BlockSpec((STEP, size, HALF), lambda s, *_: (jnp.minimum(s, steps - 1), h, 0))


def forward(pair, parts, tokens):
    steps = [piece["count"] // STEP for piece in pair]
    operands = [piece[key] for piece in pair for key in ("kept", "came")]
    size = HALF // parts
    return pl.pallas_call(
        functools.partial(forward_kernel, steps, parts),
        out_shape=[
            jax.ShapeDtypeStruct((piece["count"], size, HALF), BF16)
            for piece in pair
            for _ in range(parts)
        ],
        grid=(max(steps),),
        in_specs=[quadrant(0, steps[k // 2]) for k in range(4)] + [ANYWHERE] * len(tokens),
        out_specs=[plain(steps[k], size) for k in range(2) for _ in range(parts)],
        compiler_params=PARAMS,
        name="forward",
    )(*operands, *tokens)


def zero_kernel(_, out):
    out[...] = jnp.zeros_like(out)


def zero_buffer(count, token):
    return pl.pallas_call(
        zero_kernel,
        out_shape=jax.ShapeDtypeStruct((count, HALF, HALF), BF16),
        grid=(count // 64,),
        in_specs=[ANYWHERE],
        out_specs=pl.BlockSpec((64, HALF, HALF), lambda s: (s, 0, 0)),
        compiler_params=PARAMS,
        name="zero_buffer",
    )(token)


def store_roots(raw, scale):
    half = raw.shape[0] // 2
    total = raw[:half] + raw[half:]
    roots = 1.0 / jnp.sqrt(1.0 + total / (total.shape[0] * total.shape[1]))
    scale[0] = roots[:, :HALF]
    scale[1] = roots[:, HALF:]


def upright(line):
    return jnp.broadcast_to(line, (HALF, HALF)).T


def finish_kernel(starts, counts, h, index_ref, place_ref, *refs):
    total_pieces = len(starts)
    raw = refs[3 * total_pieces]
    out, scale, row_scale, col_scale, done, sem = refs[-6:]
    tiles_row, size, _ = row_scale.shape
    tiles_col = col_scale.shape[0]
    step = pl.program_id(0)

    @pl.when(step == 0)
    def _():
        row_side, row_group, col_side, col_group = position()
        store_roots(raw, scale)
        for i in range(tiles_row):
            column = upright(scale[row_side, pl.ds(row_group * tiles_row + i, 1), :])
            row_scale[i] = column[h * size : (h + 1) * size]
        for j in range(tiles_col):
            line = scale[col_side, pl.ds(col_group * tiles_col + j, 1), :]
            col_scale[j] = jnp.broadcast_to(line, (8, HALF))

    base = 0
    for number in range(total_pieces):
        kept, came, last = refs[3 * number : 3 * number + 3]

        @pl.when(step < counts[number] // STEP)
        def _(kept=kept, came=came, last=last, base=base, start=starts[number]):
            for t in range(STEP):
                m = step * STEP + t
                i = lax.div(index_ref[start + m], tiles_col)
                j = lax.rem(index_ref[start + m], tiles_col)
                total = kept[0, t].astype(F32) + came[0, t].astype(F32) + last[t].astype(F32)
                done[base + m] = (total * row_scale[i] * col_scale[j, 0:1]).astype(BF16)
                target = out.at[place_ref[start + m], pl.ds(h * size, size)]
                pltpu.make_async_copy(done.at[base + m], target, sem).start()

        base += counts[number]

    @pl.when(step == pl.num_programs(0) - 1)
    def _():
        sent = out.at[pl.ds(0, done.shape[0]), pl.ds(0, size)]
        pltpu.make_async_copy(done, sent, sem).wait()


def finish(pieces, h, index, place, raw, buffer, sizes, token):
    tiles_row, tiles_col = sizes
    size = HALF // len(pieces[0]["last"])
    starts = [piece["start"] for piece in pieces]
    counts = [piece["count"] for piece in pieces]
    specs, operands = [], []
    for piece in pieces:
        steps = piece["count"] // STEP
        specs += [quadrant(1, steps, size, h)] * 2 + [plain(steps, size)]
        operands += [piece["kept"], piece["came"], piece["last"][h]]
    return pl.pallas_call(
        functools.partial(finish_kernel, starts, counts, h),
        out_shape=jax.ShapeDtypeStruct(buffer.shape, BF16),
        grid_spec=pltpu.PrefetchScalarGridSpec(
            num_scalar_prefetch=2,
            grid=(max(counts) // STEP,),
            in_specs=specs + [full(raw.shape), ANYWHERE, ANYWHERE],
            out_specs=ANYWHERE,
            scratch_shapes=[
                pltpu.VMEM((2, raw.shape[0] // 2, HALF), F32),
                pltpu.VMEM((tiles_row, size, HALF), F32),
                pltpu.VMEM((tiles_col, 8, HALF), F32),
                pltpu.VMEM((sum(counts), size, HALF), BF16),
                pltpu.SemaphoreType.DMA,
            ],
        ),
        input_output_aliases={3 + len(operands): 0},
        compiler_params=PARAMS,
        name="finish",
    )(index, place, *operands, raw, buffer, token)


def join_kernel(tiles_row, lane_ref, kept, came, weight, raw, _, out, scale):
    row_side, row_group, _, _ = position()
    part = out.shape[0]
    store_roots(raw, scale)
    for t in range(part):
        merged = [
            (kept[h, t].astype(F32) + came[h, t].astype(F32)).astype(BF16) for h in range(2)
        ]
        joined = jnp.dot(
            jnp.concatenate(merged, axis=1), weight[...], preferred_element_type=F32
        )
        k = row_group * tiles_row + lane_ref[0] * part + t
        column = upright(scale[row_side, pl.ds(k, 1), :])
        out[t] = (joined * jnp.concatenate([column] * 2, axis=1)).astype(BF16)


def join_features(lane, piece, weight, raw, tiles_row, token):
    part = tiles_row // LANES
    block = pl.BlockSpec((2, part, HALF, HALF), lambda s, *_: (0, piece["count"] // part, 0, 0))
    shape = (part, HALF, weight.shape[1])
    return pl.pallas_call(
        functools.partial(join_kernel, tiles_row),
        out_shape=jax.ShapeDtypeStruct(shape, BF16),
        grid_spec=pltpu.PrefetchScalarGridSpec(
            num_scalar_prefetch=1,
            grid=(1,),
            in_specs=[block, block, full(weight.shape), full(raw.shape), ANYWHERE],
            out_specs=full(shape),
            scratch_shapes=[pltpu.VMEM((2, raw.shape[0] // 2, HALF), F32)],
        ),
        compiler_params=PARAMS,
        name="join_features",
    )(lane, piece["kept"], piece["came"], weight, raw, token)


def copy_kernel(pieces, *refs):
    source, shared = refs[0], refs[1 : 1 + LANES]
    out, features, held, sem, in_sem, out_sem = refs[1 + LANES :]
    size = source.shape[0] // pieces
    part = held.shape[1]
    lane = lax.rem(lax.axis_index("col"), LANES)

    def move(k):
        window = pl.ds(k * size, size)
        return pltpu.make_async_copy(source.at[window], out.at[window], sem.at[k])

    def read(k):
        return pltpu.make_async_copy(shared[k], held.at[k], in_sem.at[k])

    def write(k):
        owner = lax.rem(lane + LANES - k, LANES)
        target = features.at[pl.ds(owner * part, part)]
        return pltpu.make_async_copy(held.at[k], target, out_sem.at[k])

    for k in range(LANES):
        read(k).start()
    for k in range(pieces):
        move(k).start()
    for k in range(LANES):
        read(k).wait()
        write(k).start()
    for k in range(pieces):
        move(k).wait()
    for k in range(LANES):
        write(k).wait()


def copied(source, shared):
    pieces = 16
    part = shared[0].shape
    return pl.pallas_call(
        functools.partial(copy_kernel, pieces),
        out_shape=[
            jax.ShapeDtypeStruct(source.shape, source.dtype),
            jax.ShapeDtypeStruct((LANES * part[0],) + part[1:], BF16),
        ],
        in_specs=[ANYWHERE] * (1 + LANES),
        out_specs=[ANYWHERE, ANYWHERE],
        scratch_shapes=[
            pltpu.VMEM((LANES,) + part, BF16),
            pltpu.SemaphoreType.DMA((pieces,)),
            pltpu.SemaphoreType.DMA((LANES,)),
            pltpu.SemaphoreType.DMA((LANES,)),
        ],
        compiler_params=pltpu.CompilerParams(vmem_limit_bytes=2 << 20),
        name="copied",
    )(source, *shared)


def level(features, join_weight, partner, tile_index, tile_values, pert_slot, pert_values, routes):
    row_count = lax.axis_size("row")
    col_count = lax.axis_size("col")
    devices = row_count * col_count
    masks = ("row", row_count // 2), ("col", col_count // 2)
    slot_count = tile_values.shape[0]
    width = features.shape[1]
    tiles_row = features.shape[0] // TILE
    tiles_col = partner.shape[0] // TILE // col_count
    sizes = tiles_row, tiles_col
    capacity = routes.shape[1]
    chunks = len(CHUNKS)
    lane = (lax.axis_index("col") % LANES).reshape(1)
    partner = partner.reshape(-1, HALF)
    feature_tiles = features.reshape(tiles_row, TILE, width)

    starts = [0, ROW_FIRST]
    token = pert_values
    pairs = []
    for chunk in range(chunks):
        counts = CHUNKS[chunk]
        row_given, row_kept, col_given, col_kept = pair_tiles(
            tuple(starts), counts, tile_index, pert_slot, lane, tile_values, partner,
            pert_values, feature_tiles if chunk == 0 else None, sizes, token,
        )
        token = col_kept
        pair = []
        for kind, (given, kept) in enumerate(((row_given, row_kept), (col_given, col_kept))):
            came = flipped(given, *masks[kind])
            pair.append(
                dict(
                    row_first=kind == 0, start=starts[kind], count=counts[kind],
                    given=given, kept=kept, came=came,
                )
            )
            starts[kind] += counts[kind]
        pairs.append(pair)

    own = sum_rows([piece for pair in pairs for piece in pair], tile_index, sizes)
    spread = lax.all_to_all(own, "col", split_axis=0, concat_axis=0, tiled=True)

    targets = routes[:, 0]
    order = jnp.arange(slot_count, dtype=jnp.int32)
    same = (targets[:, None] == targets[None, :]) & (order[None, :] < order[:, None])
    place = targets * capacity + jnp.sum(same.astype(jnp.int32), axis=1)

    buffer = zero_buffer(devices * capacity, own)
    token = buffer
    for chunk, pair in enumerate(pairs):
        splits = SPLITS[chunk]
        given = forward(pair, splits, [token, place] if chunk == 0 else [token])
        token = given[0]
        for kind in range(2):
            pair[kind]["last"] = []
            for h in range(splits):
                last = flipped(given[kind * splits + h], *masks[1 - kind])
                pair[kind]["last"].append(last)
        if chunk == 1:
            token = line_copies(spread, devices, token)
            raw = lax.all_to_all(token, ("row", "col"), split_axis=0, concat_axis=0, tiled=True)

    joined = join_features(lane, pairs[0][0], join_weight, raw, tiles_row, token)
    shared = [joined]
    for shift in range(1, LANES):
        ring = [
            (source, source // LANES * LANES + (source + shift) % LANES)
            for source in range(col_count)
        ]
        shared.append(lax.ppermute(joined, "col", ring))
    for chunk, pair in enumerate(pairs):
        for h in range(SPLITS[chunk]):
            buffer = finish(pair, h, tile_index, place, raw, buffer, sizes, joined)
    arrived = lax.all_to_all(buffer, ("row", "col"), split_axis=0, concat_axis=0, tiled=True)
    result, coarse_features = copied(arrived, shared)
    return (coarse_features.reshape(tiles_row * HALF, width), result)


def solution(mesh):
    both = P(("row", "col"))
    placed = (
        P("row", None),
        P(),
        P(),
        both,
        P(("row", "col"), None, None),
        both,
        P(("row", "col"), None, None),
        P(("row", "col"), None),
    )
    return jax.shard_map(
        level,
        mesh=mesh,
        in_specs=placed,
        out_specs=(P("row", None), P(("row", "col"), None, None)),
        check_vma=False,
    )
```

```python
import functools

import jax
import jax.numpy as jnp
from jax import lax
from jax.experimental import pallas as pl
from jax.experimental.pallas import tpu as pltpu
from jax.sharding import PartitionSpec as P


TILE = 256
HALF = 128
STEP = 8
LANES = 4
ROW_FIRST = 48
CHUNKS = (8, 8), (8, 16), (16, 16), (16, 16)
SPLITS = 1, 1, 1, 1
BF16 = jnp.bfloat16
F32 = jnp.float32
PARAMS = pltpu.CompilerParams(vmem_limit_bytes=66_500_000)
ANYWHERE = pl.BlockSpec(memory_space=pl.ANY)


def flipped(value, axis, mask):
    pairs = [(source, source ^ mask) for source in range(lax.axis_size(axis))]
    return lax.ppermute(value, axis, pairs)


def full(shape):
    return pl.BlockSpec(shape, lambda *_: (0,) * len(shape))


def iota(shape, axis):
    return lax.broadcasted_iota(jnp.int32, shape, axis)


def position():
    row_half = lax.axis_size("row") // 2
    col_half = lax.axis_size("col") // 2
    row_index = lax.axis_index("row")
    col_index = lax.axis_index("col")
    return (
        lax.div(row_index, row_half),
        lax.rem(row_index, row_half),
        lax.div(col_index, col_half),
        lax.rem(col_index, col_half),
    )


def build_tables(partner_ref, row_tables, col_tables):
    row_side, row_group, col_side, col_group = position()
    tiles_row = row_tables.shape[0]
    tiles_col = col_tables.shape[0]
    coarse_nodes = partner_ref.shape[0] * HALF // 2
    rotated = (iota((1, TILE), 1) + HALF) & (TILE - 1)
    level = iota((TILE, TILE), 0).astype(F32).astype(BF16)

    def vector(start, shift):
        first = partner_ref[pl.ds(start, 1), :]
        second = partner_ref[pl.ds(start + 1, 1), :]
        return jnp.concatenate([first, second], axis=1) - shift

    def table(values):
        line = values.astype(F32).astype(BF16)
        same = jnp.broadcast_to(line, (TILE, TILE)) == level
        return jnp.where(same, jnp.ones((), BF16), jnp.zeros((), BF16))

    for i in range(tiles_row):
        k = row_group * tiles_row + i
        slots = vector(coarse_nodes // HALF + 2 * k, k * TILE)
        row_tables[i] = table(jnp.where(row_side == 1, slots, rotated))
    for j in range(tiles_col):
        k = col_group * tiles_col + j
        nodes = vector(2 * k, coarse_nodes + k * TILE)
        col_tables[j] = table(jnp.where(col_side == 1, nodes, rotated))


def pair_kernel(
    starts, counts, with_features, index_ref, pert_ref, lane_ref, tiles, partner_ref, perts, *rest
):
    if with_features:
        features, rest = rest[0], rest[1:]
    _, row_given, row_kept, col_given, col_kept, row_tables, col_tables, rows = rest
    tiles_col = col_tables.shape[0]
    step = pl.program_id(0)
    row_steps = counts[0] // STEP
    pert_count = pert_ref.shape[0]
    first = jnp.where(
        step < row_steps, starts[0] + step * STEP, starts[1] + (step - row_steps) * STEP
    )

    @pl.when(step == 0)
    def _():
        build_tables(partner_ref, row_tables, col_tables)

    hits = sum(
        ((pert_ref[p] >= first) & (pert_ref[p] < first + STEP)).astype(jnp.int32)
        for p in range(pert_count)
    )

    @pl.when(hits > 0)
    def _():
        for t in range(STEP):
            found = sum((pert_ref[p] == first + t).astype(jnp.int32) for p in range(pert_count))

            @pl.when(found > 0)
            def _():
                total = tiles[t].astype(F32)
                for p in range(pert_count):
                    total = total + jnp.where(pert_ref[p] == first + t, perts[p].astype(F32), 0.0)
                tiles[t] = total.astype(BF16)

    def put(t, both, given, kept, row_first):
        cross = both[:HALF, HALF:], both[HALF:, :HALF]
        given[0, t] = both[:HALF, :HALF]
        given[1, t] = cross[0 if row_first else 1]
        kept[0, t] = cross[1 if row_first else 0]
        kept[1, t] = both[HALF:, HALF:]

    def compute(given, kept, row_first):
        for t in range(STEP):
            i = lax.div(index_ref[first + t], tiles_col)
            rows[t] = jnp.dot(row_tables[i], tiles[t], preferred_element_type=F32).astype(BF16)
        for t in range(STEP):
            j = lax.rem(index_ref[first + t], tiles_col)
            both = jnp.dot(rows[t], col_tables[j], preferred_element_type=F32).astype(BF16)
            put(t, both, given, kept, row_first)

    @pl.when(step < row_steps)
    def _():
        compute(row_given, row_kept, True)
        if with_features:
            for t in range(features.shape[0]):
                table = row_tables[lane_ref[0] * features.shape[0] + t]
                both = jnp.dot(table, features[t], preferred_element_type=F32).astype(BF16)
                put(STEP + t, both, row_given, row_kept, True)

    @pl.when(step >= row_steps)
    def _():
        compute(col_given, col_kept, False)


def pair_tiles(
    starts, counts, index, pert_slot, lane, tile_values, partner, pert_values, features, sizes, token
):
    tiles_row, tiles_col = sizes
    row_steps, col_steps = counts[0] // STEP, counts[1] // STEP
    row_block, col_block = starts[0] // STEP, starts[1] // STEP
    with_features = features is not None
    extra = features.shape[0] // LANES if with_features else 0

    def tile_map(s, *_):
        return (jnp.where(s < row_steps, row_block + s, col_block + s - row_steps), 0, 0)

    shapes = [
        jax.ShapeDtypeStruct((2, count, HALF, HALF), BF16)
        for count in (counts[0] + extra,) * 2 + (counts[1],) * 2
    ]
    if with_features:
        row_out = full(shapes[0].shape)
    else:
        row_out = pl.BlockSpec(
            (2, STEP, HALF, HALF), lambda s, *_: (0, jnp.minimum(s, row_steps - 1), 0, 0)
        )
    col_out = pl.BlockSpec(
        (2, STEP, HALF, HALF), lambda s, *_: (0, jnp.maximum(s - row_steps, 0), 0, 0)
    )
    in_specs = [
        pl.BlockSpec((STEP, TILE, TILE), tile_map),
        full(partner.shape),
        full(pert_values.shape),
    ]
    operands = [tile_values, partner, pert_values]
    if with_features:
        in_specs.append(
            pl.BlockSpec((extra,) + features.shape[1:], lambda s, a, b, lane: (lane[0], 0, 0))
        )
        operands.append(features)
    return pl.pallas_call(
        functools.partial(pair_kernel, starts, counts, with_features),
        out_shape=shapes,
        grid_spec=pltpu.PrefetchScalarGridSpec(
            num_scalar_prefetch=3,
            grid=(row_steps + col_steps,),
            in_specs=in_specs + [ANYWHERE],
            out_specs=[row_out, row_out, col_out, col_out],
            scratch_shapes=[
                pltpu.VMEM((tiles_row, TILE, TILE), BF16),
                pltpu.VMEM((tiles_col, TILE, TILE), BF16),
                pltpu.VMEM((STEP, TILE, TILE), BF16),
            ],
        ),
        compiler_params=PARAMS,
        name="pair_tiles",
    )(index, pert_slot, lane, *operands, token)


def sum_kernel(bounds, tiles_col, index_ref, *rest):
    pieces, sums, total = rest[:-2], rest[-2], rest[-1]
    step = pl.program_id(0)

    @pl.when(step == 0)
    def _():
        total[...] = jnp.zeros_like(total)

    for number, (begin, steps, start, row_first) in enumerate(bounds):
        given, kept = pieces[2 * number], pieces[2 * number + 1]

        @pl.when((step >= begin) & (step < begin + steps))
        def _():
            for t in range(STEP):
                i = lax.div(index_ref[start + (step - begin) * STEP + t], tiles_col)
                cross = given[1, t].astype(F32), kept[0, t].astype(F32)
                given_part, kept_part = cross if row_first else cross[::-1]
                total[0, i] += given[0, t].astype(F32) + given_part
                total[1, i] += kept[1, t].astype(F32) + kept_part

    @pl.when(step == pl.num_programs(0) - 1)
    def _():
        row_side = position()[0]
        for i in range(total.shape[1]):
            given_line = jnp.sum(total[0, i].T, axis=0, keepdims=True)
            kept_line = jnp.sum(total[1, i].T, axis=0, keepdims=True)
            sums[i : i + 1, :HALF] = jnp.where(row_side == 1, given_line, kept_line)
            sums[i : i + 1, HALF:] = jnp.where(row_side == 1, kept_line, given_line)


def sum_rows(pieces, index, sizes):
    tiles_row, tiles_col = sizes
    bounds, specs, operands = [], [], []
    begin = 0
    for piece in pieces:
        steps = piece["count"] // STEP

        def block_map(s, *_, begin=begin, steps=steps):
            return (0, jnp.clip(s - begin, 0, steps - 1), 0, 0)

        specs += [pl.BlockSpec((2, STEP, HALF, HALF), block_map)] * 2
        operands += [piece["given"], piece["kept"]]
        bounds.append((begin, steps, piece["start"], piece["row_first"]))
        begin += steps
    return pl.pallas_call(
        functools.partial(sum_kernel, bounds, tiles_col),
        out_shape=jax.ShapeDtypeStruct((tiles_row, TILE), F32),
        grid_spec=pltpu.PrefetchScalarGridSpec(
            num_scalar_prefetch=1,
            grid=(begin,),
            in_specs=specs,
            out_specs=full((tiles_row, TILE)),
            scratch_shapes=[pltpu.VMEM((2, tiles_row, HALF, HALF), F32)],
        ),
        compiler_params=PARAMS,
        name="sum_rows",
    )(index, *operands)


def line_kernel(spread, _, out):
    line = jnp.sum(spread[...], axis=0, keepdims=True)
    out[...] = jnp.broadcast_to(line, out.shape)


def line_copies(spread, devices, token):
    return pl.pallas_call(
        line_kernel,
        out_shape=jax.ShapeDtypeStruct((devices, TILE), F32),
        in_specs=[pl.BlockSpec(memory_space=pltpu.VMEM), ANYWHERE],
        out_specs=pl.BlockSpec(memory_space=pltpu.VMEM),
        compiler_params=PARAMS,
        name="line_copies",
    )(spread, token)


def forward_kernel(steps, parts, *refs):
    row_kept, row_came, col_kept, col_came = refs[:4]
    row_given, col_given = refs[-2 * parts : -parts], refs[-parts:]
    step = pl.program_id(0)
    size = HALF // parts

    def both(kept, came, given):
        total = (kept[0].astype(F32) + came[0].astype(F32)).astype(BF16)
        for h in range(parts):
            given[h][...] = total[:, h * size : (h + 1) * size]

    pl.when(step < steps[0])(lambda: both(row_kept, row_came, row_given))
    pl.when(step < steps[1])(lambda: both(col_kept, col_came, col_given))


def quadrant(which, steps, size=HALF, h=0):
    return pl.BlockSpec(
        (1, STEP, size, HALF), lambda s, *_: (which, jnp.minimum(s, steps - 1), h, 0)
    )


def plain(steps, size=HALF, h=0):
    return pl.BlockSpec((STEP, size, HALF), lambda s, *_: (jnp.minimum(s, steps - 1), h, 0))


def forward(pair, parts, tokens):
    steps = [piece["count"] // STEP for piece in pair]
    operands = [piece[key] for piece in pair for key in ("kept", "came")]
    size = HALF // parts
    return pl.pallas_call(
        functools.partial(forward_kernel, steps, parts),
        out_shape=[
            jax.ShapeDtypeStruct((piece["count"], size, HALF), BF16)
            for piece in pair
            for _ in range(parts)
        ],
        grid=(max(steps),),
        in_specs=[quadrant(0, steps[k // 2]) for k in range(4)] + [ANYWHERE] * len(tokens),
        out_specs=[plain(steps[k], size) for k in range(2) for _ in range(parts)],
        compiler_params=PARAMS,
        name="forward",
    )(*operands, *tokens)


def zero_kernel(_, out):
    out[...] = jnp.zeros_like(out)


def zero_buffer(count, token):
    return pl.pallas_call(
        zero_kernel,
        out_shape=jax.ShapeDtypeStruct((count, HALF, HALF), BF16),
        grid=(count // 64,),
        in_specs=[ANYWHERE],
        out_specs=pl.BlockSpec((64, HALF, HALF), lambda s: (s, 0, 0)),
        compiler_params=PARAMS,
        name="zero_buffer",
    )(token)


def store_roots(raw, scale):
    half = raw.shape[0] // 2
    total = raw[:half] + raw[half:]
    roots = 1.0 / jnp.sqrt(1.0 + total / (total.shape[0] * total.shape[1]))
    scale[0] = roots[:, :HALF]
    scale[1] = roots[:, HALF:]


def upright(line):
    return jnp.broadcast_to(line, (HALF, HALF)).T


def finish_kernel(starts, counts, h, index_ref, place_ref, *refs):
    total_pieces = len(starts)
    raw = refs[3 * total_pieces]
    out, scale, row_scale, col_scale, done, sem = refs[-6:]
    tiles_row, size, _ = row_scale.shape
    tiles_col = col_scale.shape[0]
    step = pl.program_id(0)

    @pl.when(step == 0)
    def _():
        row_side, row_group, col_side, col_group = position()
        store_roots(raw, scale)
        for i in range(tiles_row):
            column = upright(scale[row_side, pl.ds(row_group * tiles_row + i, 1), :])
            row_scale[i] = column[h * size : (h + 1) * size]
        for j in range(tiles_col):
            line = scale[col_side, pl.ds(col_group * tiles_col + j, 1), :]
            col_scale[j] = jnp.broadcast_to(line, (8, HALF))

    base = 0
    for number in range(total_pieces):
        kept, came, last = refs[3 * number : 3 * number + 3]

        @pl.when(step < counts[number] // STEP)
        def _(kept=kept, came=came, last=last, base=base, start=starts[number]):
            for t in range(STEP):
                m = step * STEP + t
                i = lax.div(index_ref[start + m], tiles_col)
                j = lax.rem(index_ref[start + m], tiles_col)
                total = kept[0, t].astype(F32) + came[0, t].astype(F32) + last[t].astype(F32)
                done[base + m] = (total * row_scale[i] * col_scale[j, 0:1]).astype(BF16)
                target = out.at[place_ref[start + m], pl.ds(h * size, size)]
                pltpu.make_async_copy(done.at[base + m], target, sem).start()

        base += counts[number]

    @pl.when(step == pl.num_programs(0) - 1)
    def _():
        sent = out.at[pl.ds(0, done.shape[0]), pl.ds(0, size)]
        pltpu.make_async_copy(done, sent, sem).wait()


def finish(pieces, h, index, place, raw, buffer, sizes, token):
    tiles_row, tiles_col = sizes
    size = HALF // len(pieces[0]["last"])
    starts = [piece["start"] for piece in pieces]
    counts = [piece["count"] for piece in pieces]
    specs, operands = [], []
    for piece in pieces:
        steps = piece["count"] // STEP
        specs += [quadrant(1, steps, size, h)] * 2 + [plain(steps, size)]
        operands += [piece["kept"], piece["came"], piece["last"][h]]
    return pl.pallas_call(
        functools.partial(finish_kernel, starts, counts, h),
        out_shape=jax.ShapeDtypeStruct(buffer.shape, BF16),
        grid_spec=pltpu.PrefetchScalarGridSpec(
            num_scalar_prefetch=2,
            grid=(max(counts) // STEP,),
            in_specs=specs + [full(raw.shape), ANYWHERE, ANYWHERE],
            out_specs=ANYWHERE,
            scratch_shapes=[
                pltpu.VMEM((2, raw.shape[0] // 2, HALF), F32),
                pltpu.VMEM((tiles_row, size, HALF), F32),
                pltpu.VMEM((tiles_col, 8, HALF), F32),
                pltpu.VMEM((sum(counts), size, HALF), BF16),
                pltpu.SemaphoreType.DMA,
            ],
        ),
        input_output_aliases={3 + len(operands): 0},
        compiler_params=PARAMS,
        name="finish",
    )(index, place, *operands, raw, buffer, token)


def join_kernel(tiles_row, lane_ref, kept, came, weight, raw, _, out, scale):
    row_side, row_group, _, _ = position()
    part = out.shape[0]
    store_roots(raw, scale)
    for t in range(part):
        merged = [
            (kept[h, t].astype(F32) + came[h, t].astype(F32)).astype(BF16) for h in range(2)
        ]
        joined = jnp.dot(
            jnp.concatenate(merged, axis=1), weight[...], preferred_element_type=F32
        )
        k = row_group * tiles_row + lane_ref[0] * part + t
        column = upright(scale[row_side, pl.ds(k, 1), :])
        out[t] = (joined * jnp.concatenate([column] * 2, axis=1)).astype(BF16)


def join_features(lane, piece, weight, raw, tiles_row, token):
    part = tiles_row // LANES
    block = pl.BlockSpec((2, part, HALF, HALF), lambda s, *_: (0, piece["count"] // part, 0, 0))
    shape = (part, HALF, weight.shape[1])
    return pl.pallas_call(
        functools.partial(join_kernel, tiles_row),
        out_shape=jax.ShapeDtypeStruct(shape, BF16),
        grid_spec=pltpu.PrefetchScalarGridSpec(
            num_scalar_prefetch=1,
            grid=(1,),
            in_specs=[block, block, full(weight.shape), full(raw.shape), ANYWHERE],
            out_specs=full(shape),
            scratch_shapes=[pltpu.VMEM((2, raw.shape[0] // 2, HALF), F32)],
        ),
        compiler_params=PARAMS,
        name="join_features",
    )(lane, piece["kept"], piece["came"], weight, raw, token)


def copy_kernel(pieces, *refs):
    source, shared = refs[0], refs[1 : 1 + LANES]
    out, features, held, sem, in_sem, out_sem = refs[1 + LANES :]
    size = source.shape[0] // pieces
    part = held.shape[1]
    lane = lax.rem(lax.axis_index("col"), LANES)

    def move(k):
        window = pl.ds(k * size, size)
        return pltpu.make_async_copy(source.at[window], out.at[window], sem.at[k])

    def read(k):
        return pltpu.make_async_copy(shared[k], held.at[k], in_sem.at[k])

    def write(k):
        owner = lax.rem(lane + LANES - k, LANES)
        target = features.at[pl.ds(owner * part, part)]
        return pltpu.make_async_copy(held.at[k], target, out_sem.at[k])

    for k in range(LANES):
        read(k).start()
    for k in range(pieces):
        move(k).start()
    for k in range(LANES):
        read(k).wait()
        write(k).start()
    for k in range(pieces):
        move(k).wait()
    for k in range(LANES):
        write(k).wait()


def copied(source, shared):
    pieces = 16
    part = shared[0].shape
    return pl.pallas_call(
        functools.partial(copy_kernel, pieces),
        out_shape=[
            jax.ShapeDtypeStruct(source.shape, source.dtype),
            jax.ShapeDtypeStruct((LANES * part[0],) + part[1:], BF16),
        ],
        in_specs=[ANYWHERE] * (1 + LANES),
        out_specs=[ANYWHERE, ANYWHERE],
        scratch_shapes=[
            pltpu.VMEM((LANES,) + part, BF16),
            pltpu.SemaphoreType.DMA((pieces,)),
            pltpu.SemaphoreType.DMA((LANES,)),
            pltpu.SemaphoreType.DMA((LANES,)),
        ],
        compiler_params=pltpu.CompilerParams(vmem_limit_bytes=2 << 20),
        name="copied",
    )(source, *shared)


def level(features, join_weight, partner, tile_index, tile_values, pert_slot, pert_values, routes):
    row_count = lax.axis_size("row")
    col_count = lax.axis_size("col")
    devices = row_count * col_count
    masks = ("row", row_count // 2), ("col", col_count // 2)
    slot_count = tile_values.shape[0]
    width = features.shape[1]
    tiles_row = features.shape[0] // TILE
    tiles_col = partner.shape[0] // TILE // col_count
    sizes = tiles_row, tiles_col
    capacity = routes.shape[1]
    chunks = len(CHUNKS)
    lane = (lax.axis_index("col") % LANES).reshape(1)
    partner = partner.reshape(-1, HALF)
    feature_tiles = features.reshape(tiles_row, TILE, width)

    starts = [0, ROW_FIRST]
    token = pert_values
    pairs = []
    for chunk in range(chunks):
        counts = CHUNKS[chunk]
        row_given, row_kept, col_given, col_kept = pair_tiles(
            tuple(starts), counts, tile_index, pert_slot, lane, tile_values, partner,
            pert_values, feature_tiles if chunk == 0 else None, sizes, token,
        )
        token = col_kept
        pair = []
        for kind, (given, kept) in enumerate(((row_given, row_kept), (col_given, col_kept))):
            came = flipped(given, *masks[kind])
            pair.append(
                dict(
                    row_first=kind == 0, start=starts[kind], count=counts[kind],
                    given=given, kept=kept, came=came,
                )
            )
            starts[kind] += counts[kind]
        pairs.append(pair)

    own = sum_rows([piece for pair in pairs for piece in pair], tile_index, sizes)
    spread = lax.all_to_all(own, "col", split_axis=0, concat_axis=0, tiled=True)

    targets = routes[:, 0]
    order = jnp.arange(slot_count, dtype=jnp.int32)
    same = (targets[:, None] == targets[None, :]) & (order[None, :] < order[:, None])
    place = targets * capacity + jnp.sum(same.astype(jnp.int32), axis=1)

    buffer = zero_buffer(devices * capacity, own)
    token = buffer
    for chunk, pair in enumerate(pairs):
        splits = SPLITS[chunk]
        given = forward(pair, splits, [token, place] if chunk == 0 else [token])
        token = given[0]
        for kind in range(2):
            pair[kind]["last"] = []
            for h in range(splits):
                last = flipped(given[kind * splits + h], *masks[1 - kind])
                pair[kind]["last"].append(last)
        if chunk == 1:
            token = line_copies(spread, devices, token)
            raw = lax.all_to_all(token, ("row", "col"), split_axis=0, concat_axis=0, tiled=True)

    joined = join_features(lane, pairs[0][0], join_weight, raw, tiles_row, token)
    shared = [joined]
    for shift in range(1, LANES):
        ring = [
            (source, source // LANES * LANES + (source + shift) % LANES)
            for source in range(col_count)
        ]
        shared.append(lax.ppermute(joined, "col", ring))
    groups = [pairs[0] + pairs[1]] + pairs[2:]
    for group in groups:
        buffer = finish(group, 0, tile_index, place, raw, buffer, sizes, joined)
    arrived = lax.all_to_all(buffer, ("row", "col"), split_axis=0, concat_axis=0, tiled=True)
    result, coarse_features = copied(arrived, shared)
    return (coarse_features.reshape(tiles_row * HALF, width), result)


def solution(mesh):
    both = P(("row", "col"))
    placed = (
        P("row", None),
        P(),
        P(),
        both,
        P(("row", "col"), None, None),
        both,
        P(("row", "col"), None, None),
        P(("row", "col"), None),
    )
    return jax.shard_map(
        level,
        mesh=mesh,
        in_specs=placed,
        out_specs=(P("row", None), P(("row", "col"), None, None)),
        check_vma=False,
    )
```
